128 devices in a mesh: dp: 2 (over core), seq: 64 (over z, y, x).
Axes of the slice: x: 4, y: 4, z: 4, core: 2. Of those that a mesh axis runs over, the one named last changes fastest.
Arguments:
- queries: bfloat16 [65536, 1024], P(('dp', 'seq')), may hold values from -20 to 20
- keys: bfloat16 [65536, 1024], P(('dp', 'seq')), may hold values from -12 to 12
- value_sel: bfloat16 [65536, 4, 2, 256], P(('dp', 'seq')), may hold values from -6 to 6
- expert_logits: float32 [65536, 4, 16], P(('dp', 'seq')), may hold values from -8 to 8
- expert_index: int32 [65536, 4, 2], P(('dp', 'seq')), may hold values from 0 to 15, all different within a row
- doc_lengths: int32 [2, 64], P('dp'), may hold values from 1 to 1536, 32768 in all within a row
- group_plan: int32 [2], replicated, may hold values from 0 to 1, each once
- grad_attended: bfloat16 [65536, 1024], P(('dp', 'seq')), may hold values from -6 to 6
Outputs:
- attended: bfloat16 [65536, 1024], P(('dp', 'seq'))
- grad_queries: bfloat16 [65536, 1024], P(('dp', 'seq'))
- grad_keys: bfloat16 [65536, 1024], P(('dp', 'seq'))
- grad_value_sel: bfloat16 [65536, 4, 2, 256], P(('dp', 'seq'))
- router_logit_gradient: float32 [65536, 4, 16], P(('dp', 'seq'))
The draws below stay inside these ranges and needn't reach their ends.
Inputs may be any that keep to these rules, and one draw needn't show every extreme that they name: `doc_lengths`: each row sums to 32768; the longest document of each pack has exactly 1536 tokens. `group_plan`: a permutation of the data groups. `expert_index`: the 2 experts of a token and head differ.
All inputs are finite; a program needn't handle non-finite values.
Results may differ from the reference program's by a relative error of at most 0.006.
Values may be sent and summed in bfloat16 or wider, within the bound.
A program may use at most 128 MiB of HBM per device.

```python
import math
import jax
import jax.numpy as jnp
import numpy as np
from jax import lax

HEAD_NUMBER = 4
HEAD_WIDTH = 256
E = 16
TOP = 2
TOK_DEV = 512
PACK_TOKENS = 32768
TOKENS = 65536
NDOC = 64
N_DP = 2
N_SEQ = 64


def common_keys(key):
    drawn = jax.random.normal(jax.random.fold_in(key, 11), (TOKENS, HEAD_NUMBER * HEAD_WIDTH), jnp.float32)
    return jnp.clip(drawn, -6.0, 6.0)


def draw_keys(key, part):
    common = common_keys(key)
    return common.astype(jnp.bfloat16)


def draw_queries(key, part):
    drawn = jax.random.normal(jax.random.fold_in(key, 23), (TOKENS, HEAD_NUMBER * HEAD_WIDTH), jnp.float32)
    drawn = jnp.clip(drawn, -6.0, 6.0)
    return drawn.astype(jnp.bfloat16)


def levels(stream_key, dims, pieces, smallest, largest):
    loudness, own = 1.0, jax.random.fold_in(stream_key, 6)
    for dim, blocks in pieces:
        steps = jnp.exp(jax.random.uniform(jax.random.fold_in(own, dim), (blocks,), jnp.float32, smallest / len(pieces), largest / len(pieces)))
        loudness = loudness * jnp.repeat(steps, dims[dim] // blocks).reshape([-1 if axis == dim else 1 for axis in range(len(dims))])
    return loudness


def distinct(key, rows, number_of, top, lift):
    ranking = jax.random.permutation(jax.random.fold_in(key, 1), number_of)
    boost = ranking
    for power in range(3):
        boost = boost * boost // number_of
    boost = boost * lift // number_of
    chance = jax.random.randint(jax.random.fold_in(key, 2), (rows, number_of), 0, 4096) + boost
    fixed_rows = jax.random.permutation(jax.random.fold_in(key, 3), rows)[jnp.arange(number_of) % rows]
    chance = jnp.where(jnp.arange(rows)[:, None] == fixed_rows[None, :], 1 << 14, chance)
    merit = chance * number_of + jnp.arange(number_of)
    return lax.top_k(merit.astype(jnp.int32), top)[1].astype(jnp.int32)


def profile(amount, total, reach, lean):
    weights = [(1 << 20) // math.isqrt(standing ** lean) + 1 for standing in range(2, amount + 1)]
    surplus, counts = total - reach - (amount - 1), [1] * (amount - 1)
    while surplus > 0:
        movable = [i for i in range(amount - 1) if counts[i] < reach]
        pool, left = sum([weights[i] for i in movable]), surplus
        for i in movable:
            addition = min(reach - counts[i], max(1, left * weights[i] // pool), surplus)
            counts[i] = counts[i] + addition
            surplus = surplus - addition
    return np.array([reach] + counts)


def ragged_sizes(key, number_of, total, most, slope):
    if number_of == 2:
        one = jax.random.randint(key, (), max(1, total - most), min(most, total - 1) + 1)
        return jnp.stack([one, total - one])
    sizes = jnp.asarray(profile(number_of, total, most, slope), jnp.int32)
    twos = (number_of - 1) // 2
    donor, sink = sizes[1:1 + 2 * twos:2], sizes[2:2 + 2 * twos:2]
    margin = jnp.minimum(donor - 1, most - sink)
    shifted = jax.random.randint(jax.random.fold_in(key, 1), (twos,), 0, 1 << 20) % (margin + 1)
    sizes = sizes.at[1:1 + 2 * twos:2].set(donor - shifted).at[2:2 + 2 * twos:2].set(sink + shifted)
    return sizes[jax.random.permutation(jax.random.fold_in(key, 2), number_of)]


def centred(own_key, dims, width, limit, shards=(), kind=jnp.bfloat16):
    level = levels(own_key, dims, shards, -0.22, 0.18) if shards else 1.0
    result = jax.random.normal(own_key, dims, jnp.float32) * width * level
    return jnp.minimum(jnp.maximum(result, -limit), limit).astype(kind)


def setup_inputs(seed: int = 0) -> dict:
    arg_keys = jax.random.split(jax.random.key(seed), 9)
    queries = draw_queries(jax.random.fold_in(arg_keys[8], 71), 0)
    keys = draw_keys(jax.random.fold_in(arg_keys[8], 71), 0)
    value_sel = centred(arg_keys[2], (TOKENS, HEAD_NUMBER, TOP, HEAD_WIDTH), 1.0, 6.0, ((0, 128),))
    expert_logits = centred(arg_keys[3], (TOKENS, HEAD_NUMBER, E), 2.0, 8.0, ((0, 128),), jnp.float32)
    expert_index = distinct(arg_keys[4], TOKENS * HEAD_NUMBER, E, TOP, 2048).reshape((TOKENS, HEAD_NUMBER, TOP))
    doc_lengths = jax.vmap(lambda own: ragged_sizes(own, NDOC, PACK_TOKENS, 3 * TOK_DEV, 2))(jax.random.split(arg_keys[5], N_DP)).reshape((N_DP, NDOC)).astype(jnp.int32)
    group_plan = jax.random.permutation(arg_keys[6], N_DP).astype(jnp.int32)
    grad_attended = centred(arg_keys[7], (TOKENS, HEAD_NUMBER * HEAD_WIDTH), 1.0, 6.0, ((0, 128),))
    return {"queries": queries, "keys": keys, "value_sel": value_sel, "expert_logits": expert_logits, "expert_index": expert_index, "doc_lengths": doc_lengths, "group_plan": group_plan, "grad_attended": grad_attended}


def gate_table(expert_logits, expert_index):
    experts = expert_logits.shape[2]
    onehot = (expert_index[..., None] == jnp.arange(experts, dtype=jnp.int32)).astype(jnp.float32)
    chosen = lax.optimization_barrier(jnp.sum(onehot * expert_logits[:, :, None, :], axis=3))
    return (jax.nn.sigmoid(chosen), onehot)

def doc_index(positions, doc_ends):
    return lax.optimization_barrier(jnp.sum((doc_ends[None, :] <= positions[:, None]).astype(jnp.int32), axis=1))

def attend_block(query_blk, near_keys, near_values, grad_blk, query_pos, key_pos, doc_ends):
    scale = 1.0 / math.sqrt(query_blk.shape[2])
    allowed = doc_index(query_pos, doc_ends)[:, None] == doc_index(key_pos, doc_ends)[None, :]
    allowed = allowed & (key_pos[None, :] <= query_pos[:, None]) & (key_pos[None, :] >= 0)
    scores = jnp.einsum('qhd,khd->hqk', query_blk.astype(jnp.float32), near_keys.astype(jnp.float32)) * scale
    scores = jnp.where(allowed[None], scores, -1e+30)
    top_score = lax.optimization_barrier(jnp.max(scores, axis=2, keepdims=True))
    expo = jnp.exp(scores - top_score)
    probs = expo / lax.optimization_barrier(jnp.sum(expo, axis=2, keepdims=True))
    probs_low = probs.astype(jnp.bfloat16)
    out = jnp.einsum('hqk,khd->qhd', probs_low.astype(jnp.float32), near_values.astype(jnp.float32))
    grad_f = grad_blk.astype(jnp.float32)
    dprobs = jnp.einsum('qhd,khd->hqk', grad_f, near_values.astype(jnp.float32))
    delta = lax.optimization_barrier(jnp.sum(grad_f * out, axis=2))
    dscores = (probs * (dprobs - jnp.transpose(delta)[:, :, None]) * scale).astype(jnp.bfloat16)
    query_gradient = jnp.einsum('hqk,khd->qhd', dscores.astype(jnp.float32), near_keys.astype(jnp.float32))
    key_terms = jnp.einsum('hqk,qhd->khd', dscores.astype(jnp.float32), query_blk.astype(jnp.float32))
    value_terms = jnp.einsum('hqk,qhd->khd', probs_low.astype(jnp.float32), grad_f)
    return (out.astype(jnp.bfloat16), query_gradient.astype(jnp.bfloat16), key_terms, value_terms)

def collect(terms, blocks, rows):
    shaped = terms.reshape((blocks, 4, rows) + terms.shape[2:])
    padded = jnp.concatenate([shaped, jnp.zeros((3,) + shaped.shape[1:], jnp.float32)], axis=0)
    total = padded[3:3 + blocks, 0]
    for offset in range(1, 4):
        total = total + padded[3 - offset:3 - offset + blocks, offset]
    return total.reshape((blocks * rows,) + terms.shape[2:])

def pack_terms(queries, keys, value_sel, expert_logits, expert_index, lengths, grad_attended):
    rows = TOK_DEV
    blocks = N_SEQ
    gate_weights, onehot = gate_table(expert_logits, expert_index)
    mixed = lax.optimization_barrier(jnp.sum(gate_weights[..., None] * value_sel.astype(jnp.float32), axis=2)).astype(jnp.bfloat16)
    shaped_q = queries.reshape(PACK_TOKENS, HEAD_NUMBER, HEAD_WIDTH)
    shaped_g = grad_attended.reshape(PACK_TOKENS, HEAD_NUMBER, HEAD_WIDTH)
    lead = jnp.zeros((3 * rows, HEAD_NUMBER, HEAD_WIDTH), jnp.bfloat16)
    padded_keys = jnp.concatenate([lead, keys.reshape(PACK_TOKENS, HEAD_NUMBER, HEAD_WIDTH)], axis=0)
    padded_values = jnp.concatenate([lead, mixed], axis=0)
    doc_ends = jnp.cumsum(lengths).astype(jnp.int32)

    def one_block(block_idx):
        start = (block_idx * rows).astype(jnp.int32)
        query_blk = lax.dynamic_slice_in_dim(shaped_q, start, rows, 0)
        grad_blk = lax.dynamic_slice_in_dim(shaped_g, start, rows, 0)
        near_keys = lax.dynamic_slice_in_dim(padded_keys, start, 4 * rows, 0)
        near_values = lax.dynamic_slice_in_dim(padded_values, start, 4 * rows, 0)
        query_pos = start + jnp.arange(rows, dtype=jnp.int32)
        key_pos = start - 3 * rows + jnp.arange(4 * rows, dtype=jnp.int32)
        return attend_block(query_blk, near_keys, near_values, grad_blk, query_pos, key_pos, doc_ends)
    attended, query_gradient, key_terms, value_terms = lax.map(one_block, jnp.arange(blocks, dtype=jnp.int32))
    key_gradient = collect(key_terms, blocks, rows)
    value_sum_total = collect(value_terms, blocks, rows)
    selected_value_gradient = (gate_weights[..., None] * value_sum_total[:, :, None, :]).astype(jnp.bfloat16)
    gate_grad = lax.optimization_barrier(jnp.sum(value_sum_total[:, :, None, :] * value_sel.astype(jnp.float32), axis=3))
    chosen_grad = gate_grad * gate_weights * (1.0 - gate_weights)
    router_logit_gradient = lax.optimization_barrier(jnp.sum(onehot * chosen_grad[..., None], axis=2))
    return (attended.reshape(PACK_TOKENS, HEAD_NUMBER * HEAD_WIDTH), query_gradient.reshape(PACK_TOKENS, HEAD_NUMBER * HEAD_WIDTH), key_gradient.astype(jnp.bfloat16).reshape(PACK_TOKENS, HEAD_NUMBER * HEAD_WIDTH), selected_value_gradient, router_logit_gradient)

def reference(queries, keys, value_sel, expert_logits, expert_index, doc_lengths, group_plan, grad_attended):
    results = []
    for pack in range(N_DP):
        lo = pack * PACK_TOKENS
        hi = lo + PACK_TOKENS
        results.append(pack_terms(queries[lo:hi], keys[lo:hi], value_sel[lo:hi], expert_logits[lo:hi], expert_index[lo:hi], doc_lengths[pack], grad_attended[lo:hi]))
    inverse = jnp.argsort(group_plan).astype(jnp.int32)
    finals = []
    for member in range(5):
        stacked = jnp.stack([res[member] for res in results], axis=0)
        placed = jnp.take(stacked, inverse, axis=0)
        finals.append(placed.reshape((N_DP * PACK_TOKENS,) + stacked.shape[2:]))
    return (finals[0], finals[1], finals[2], finals[3], finals[4])
```

```python
import functools
import math

import jax
import jax.numpy as jnp
from jax import lax
from jax.experimental import pallas as pl
from jax.experimental.pallas import tpu as pltpu
from jax.sharding import PartitionSpec as P

MESH = pl.DeviceIdType.MESH
ANY = pl.BlockSpec(memory_space=pl.ANY)
RING = 4
T = 512
D = 256
HALO = 3 * T
ROWS = RING * T
SPAN = HALO + ROWS
HALF = T // 2
BQ = 256
CK = 256


def position():
    d = lax.axis_index("dp")
    s = lax.axis_index("seq")
    rows = lax.axis_size("seq") // RING
    return d, lax.rem(s, RING), s // RING, rows


def slab(i):
    return pl.ds(pl.multiple_of(i * D, D), D)


def span(start, size):
    return pl.ds(pl.multiple_of(start, 256), size)


def greet(devices):
    barrier = pltpu.get_barrier_semaphore()
    for device in devices:
        pl.semaphore_signal(barrier, inc=1, device_id=device, device_id_type=MESH)
    pl.semaphore_wait(barrier, len(devices))


def remote(src, dst, send, recv, device):
    return pltpu.make_async_remote_copy(
        src_ref=src,
        dst_ref=dst,
        send_sem=send,
        recv_sem=recv,
        device_id=device,
        device_id_type=MESH,
    )


def gather_kernel(
    k, v, q, g, vs, lg, ix,
    kh, vh, qh, gh, vs_p, lg_p, ix_p,
    stage, xs, xr, hs, hr, ls, lo, ps, pr,
):
    d, x, r, rows = position()
    peers = {o: (d, r * RING + lax.rem(x + o, RING)) for o in (1, 2, 3)}
    down = (d, lax.rem(r + 1, rows) * RING + x)
    up = (d, lax.rem(r + rows - 1, rows) * RING + x)
    partner = (1 - d, r * RING + x)
    greet([peers[1], peers[2], peers[3], down, up, partner])

    srcs = (k, v, q, g)
    dsts = (kh, vh, qh, gh)
    bases = (HALO, HALO, 0, 0)
    waits = []

    def x_copy(a, o, c):
        return remote(
            srcs[a].at[pl.ds(c * HALF, HALF), slab(lax.rem(x + o, RING))],
            dsts[a].at[span(bases[a] + x * T + c * HALF, HALF), :],
            xs.at[a, o - 1, c],
            xr.at[a, o - 1, c],
            peers[o],
        )

    def halo_copy(a, j, c, own):
        src = (
            srcs[a].at[pl.ds(c * HALF, HALF), slab(x)]
            if own
            else dsts[a].at[span(HALO + j * T + c * HALF, HALF), :]
        )
        return remote(
            src,
            dsts[a].at[span((j - 1) * T + c * HALF, HALF), :],
            hs.at[a, j - 1, c],
            hr.at[a, j - 1, c],
            down,
        )

    for a in (0, 1):
        for c in (0, 1):
            for o in (2, 1, 3):
                x_copy(a, o, c).start()
    for a in (0, 1):
        for c in (0, 1):
            for j in (1, 2, 3):

                @pl.when(x == j)
                def _():
                    halo_copy(a, j, c, True).start()

    for a in (2, 3):
        for c in (0, 1):
            for o in (2, 1, 3):
                x_copy(a, o, c).start()
    loads = [pltpu.make_async_copy(srcs[a].at[:, slab(x)], stage.at[a], ls.at[a]) for a in range(4)]
    for load in loads:
        load.start()
    swaps = [
        remote(src, dst, ps.at[i], pr.at[i], partner)
        for i, (src, dst) in enumerate(((vs, vs_p), (lg, lg_p), (ix, ix_p)))
    ]
    for swap in swaps:
        swap.start()
    stores = [
        pltpu.make_async_copy(
            stage.at[a], dsts[a].at[span(bases[a] + x * T, T), :], lo.at[a]
        )
        for a in range(4)
    ]
    for a in range(4):
        loads[a].wait()
        stores[a].start()

    for a in (0, 1):
        for c in (0, 1):
            for o in (1, 3, 2):
                x_copy(a, o, c).wait_recv()
                sender = lax.rem(x + RING - o, RING)
                for j in (1, 2, 3):

                    @pl.when(sender == j)
                    def _():
                        halo_copy(a, j, c, False).start()

    for a in (2, 3):
        for c in (0, 1):
            for o in (1, 3, 2):
                x_copy(a, o, c).wait_recv()
    for a in range(4):
        stores[a].wait()
        for c in (0, 1):
            for o in (1, 2, 3):
                x_copy(a, o, c).wait_send()
    for a in (0, 1):
        for c in (0, 1):
            for j in (1, 2, 3):
                halo_copy(a, j, c, False).wait()
    for swap in swaps:
        swap.wait()


def gather(k, v, q, g, vs, lg, ix):
    bf = jnp.bfloat16
    shapes = (
        jax.ShapeDtypeStruct((SPAN, D), bf),
        jax.ShapeDtypeStruct((SPAN, D), bf),
        jax.ShapeDtypeStruct((ROWS, D), bf),
        jax.ShapeDtypeStruct((ROWS, D), bf),
        jax.ShapeDtypeStruct(vs.shape, vs.dtype),
        jax.ShapeDtypeStruct(lg.shape, lg.dtype),
        jax.ShapeDtypeStruct(ix.shape, ix.dtype),
    )
    dma = pltpu.SemaphoreType.DMA
    return pl.pallas_call(
        gather_kernel,
        out_shape=shapes,
        in_specs=[ANY] * 7,
        out_specs=[ANY] * 7,
        scratch_shapes=[
            pltpu.VMEM((4, T, D), bf),
            dma((4, 3, 2)), dma((4, 3, 2)),
            dma((2, 3, 2)), dma((2, 3, 2)),
            dma((4,)), dma((4,)), dma((3,)), dma((3,)),
        ],
        compiler_params=pltpu.CompilerParams(collective_id=0, has_side_effects=True),
    )(k, v, q, g, vs, lg, ix)


def nt(a, b):
    return lax.dot_general(a, b, (((1,), (1,)), ((), ())), preferred_element_type=jnp.float32)


def nn(a, b):
    return lax.dot_general(a, b, (((1,), (0,)), ((), ())), preferred_element_type=jnp.float32)


def tn(a, b):
    return lax.dot_general(a, b, (((0,), (0,)), ((), ())), preferred_element_type=jnp.float32)


def attend_kernel(
    starts_ref, q_ref, g_ref, k_ref, v_ref,
    o_ref, dq_ref, dk_ref, dv_ref, dkh_ref, dvh_ref,
    dk_acc, dv_acc,
):
    step = pl.program_id(0)
    scale = 1.0 / math.sqrt(D)

    @pl.when(step == 0)
    def _():
        dk_acc[...] = jnp.zeros_like(dk_acc)
        dv_acc[...] = jnp.zeros_like(dv_acc)

    first = HALO + step * BQ
    starts = starts_ref[...]
    lowest = jnp.max(jnp.where(starts <= first, starts, 0))
    chunk = lowest // CK
    count = (first + BQ) // CK - chunk
    t_col = first + lax.broadcasted_iota(jnp.int32, (BQ, starts.shape[1]), 0)
    begin = jnp.max(jnp.where(starts <= t_col, starts, 0), axis=1, keepdims=True)
    t_one = first + lax.broadcasted_iota(jnp.int32, (BQ, 1), 0)

    def body(n):
        ks = pl.multiple_of(chunk * CK, CK)
        q = q_ref[...]
        g = g_ref[...]
        k = k_ref[pl.ds(ks, n * CK), :]
        v = v_ref[pl.ds(ks, n * CK), :]
        u = ks + lax.broadcasted_iota(jnp.int32, (BQ, n * CK), 1)
        s = nt(q, k) * scale
        s = jnp.where((u >= begin) & (u <= t_one), s, -1e30)
        top = jnp.max(s, axis=1, keepdims=True)
        e = jnp.exp(s - top)
        inv = 1.0 / jnp.sum(e, axis=1, keepdims=True)
        p = e * inv
        low = p.astype(jnp.bfloat16)
        o = nn(low, v)
        o_ref[...] = o.astype(jnp.bfloat16)
        delta = jnp.sum(g.astype(jnp.float32) * o, axis=1, keepdims=True)
        ds = (p * (nt(g, v) - delta) * scale).astype(jnp.bfloat16)
        dq_ref[...] = nn(ds, k).astype(jnp.bfloat16)
        dk_acc[pl.ds(ks, n * CK), :] += tn(ds, q)
        dv_acc[pl.ds(ks, n * CK), :] += tn(low, g)

    for n in range(1, HALO // CK + 2):

        @pl.when(count == n)
        def _():
            body(n)

    @pl.when(step == pl.num_programs(0) - 1)
    def _():
        dkh_ref[...] = dk_acc[:HALO, :].astype(jnp.bfloat16)
        dvh_ref[...] = dv_acc[:HALO, :].astype(jnp.bfloat16)
        dk_ref[...] = dk_acc[HALO:, :].astype(jnp.bfloat16)
        dv_ref[...] = dv_acc[HALO:, :].astype(jnp.bfloat16)


def attend(starts, q, g, k, v):
    bf = jnp.bfloat16
    tile = pl.BlockSpec((BQ, D), lambda i: (i, 0))

    def whole(rows):
        return pl.BlockSpec((rows, D), lambda i: (0, 0), pipeline_mode=pl.Buffered(1))

    return pl.pallas_call(
        attend_kernel,
        grid=(ROWS // BQ,),
        out_shape=(
            jax.ShapeDtypeStruct((ROWS, D), bf),
            jax.ShapeDtypeStruct((ROWS, D), bf),
            jax.ShapeDtypeStruct((ROWS, D), bf),
            jax.ShapeDtypeStruct((ROWS, D), bf),
            jax.ShapeDtypeStruct((HALO, D), bf),
            jax.ShapeDtypeStruct((HALO, D), bf),
        ),
        in_specs=[
            pl.BlockSpec(starts.shape, lambda i: (0, 0)),
            tile, tile, whole(SPAN), whole(SPAN),
        ],
        out_specs=[tile, tile, whole(ROWS), whole(ROWS), whole(HALO), whole(HALO)],
        scratch_shapes=[pltpu.VMEM((SPAN, D), jnp.float32)] * 2,
        compiler_params=pltpu.CompilerParams(dimension_semantics=("arbitrary",)),
    )(starts, q, g, k, v)


def home_kernel(
    swap, o, dq, dk, dv, dkh, dvh,
    att_o, dq_o, dk_o, gm_o,
    stage, own, got, xs, xr, hs, hr, ls, lo, ws,
):
    d, x, r, rows = position()
    dest = 1 - d if swap else d
    peers = {i: (dest, r * RING + lax.rem(x + i, RING)) for i in (0, 1, 2, 3)}
    down = (d, lax.rem(r + 1, rows) * RING + x)
    up = (d, lax.rem(r + rows - 1, rows) * RING + x)
    greet([peers[1], peers[2], peers[3], down, up] + ([peers[0]] if swap else []))

    halos = (dkh, dvh)
    outs = (att_o, dq_o, dk_o, gm_o)

    def halo_copy(a, j, c):
        part = pl.ds((j - 1) * T + c * HALF, HALF)
        return remote(
            halos[a].at[part, :], got.at[a, part, :], hs.at[a, j - 1, c], hr.at[a, j - 1, c], up
        )

    for c in (0, 1):
        for a in (0, 1):
            for j in (1, 2, 3):
                halo_copy(a, j, c).start()
    loads = [
        pltpu.make_async_copy(src, own.at[i], ls.at[i]) for i, src in enumerate((dk, dv))
    ]
    for load in loads:
        load.start()

    def src_of(a, block, c):
        rows_at = span(block * T + c * HALF, HALF)
        if a < 2:
            return (o, dq)[a].at[rows_at, :]
        return own.at[a - 2, rows_at, :]

    def x_copy(a, i, c):
        block = lax.rem(x + i, RING)
        return remote(
            src_of(a, block, c),
            outs[a].at[pl.ds(c * HALF, HALF), slab(x)],
            xs.at[a, i, c],
            xr.at[a, i, c],
            peers[i],
        )

    def keep(a, c):
        if a < 2:
            return pltpu.make_async_copy(
                stage.at[a, pl.ds(c * HALF, HALF), :],
                outs[a].at[pl.ds(c * HALF, HALF), slab(x)],
                lo.at[a, c],
            )
        return pltpu.make_async_copy(
            src_of(a, x, c), outs[a].at[pl.ds(c * HALF, HALF), slab(x)], lo.at[a, c]
        )

    for a in (0, 1):
        for c in (0, 1):
            for i in (2, 1, 3):
                x_copy(a, i, c).start()
    if swap:
        for a in (0, 1):
            for c in (0, 1):
                x_copy(a, 0, c).start()
    else:
        stages = [
            pltpu.make_async_copy((o, dq)[a].at[span(x * T, T), :], stage.at[a], ws.at[a])
            for a in (0, 1)
        ]
        for s in stages:
            s.start()
        for a in (0, 1):
            stages[a].wait()
            for c in (0, 1):
                keep(a, c).start()

    def send_block(a, block, c):
        for i in (0, 1, 2, 3):

            @pl.when(lax.rem(x + i, RING) == block)
            def _():
                if i == 0 and not swap:
                    keep(a, c).start()
                else:
                    x_copy(a, i, c).start()

    for load in loads:
        load.wait()
    for a in (2, 3):
        for c in (0, 1):
            send_block(a, 0, c)
    for c in (0, 1):
        for a in (0, 1):
            for j in (1, 2, 3):
                halo_copy(a, j, c).wait_recv()
                part = pl.ds((j - 1) * T + c * HALF, HALF)
                mine = pl.ds(j * T + c * HALF, HALF)
                own[a, mine, :] = (
                    own[a, mine, :].astype(jnp.float32) + got[a, part, :].astype(jnp.float32)
                ).astype(jnp.bfloat16)
                send_block(a + 2, j, c)
    for a in range(4):
        for c in (0, 1):
            for i in (1, 2, 3):
                x_copy(a, i, c).wait()
            if swap:
                x_copy(a, 0, c).wait()
            else:
                keep(a, c).wait()
    for c in (0, 1):
        for a in (0, 1):
            for j in (1, 2, 3):
                halo_copy(a, j, c).wait_send()


def home(swap, *args):
    bf = jnp.bfloat16
    dma = pltpu.SemaphoreType.DMA
    return pl.pallas_call(
        functools.partial(home_kernel, swap),
        out_shape=(jax.ShapeDtypeStruct((T, RING * D), bf),) * 4,
        in_specs=[ANY] * 6,
        out_specs=[ANY] * 4,
        scratch_shapes=[
            pltpu.VMEM((2, T, D), bf),
            pltpu.VMEM((2, ROWS, D), bf),
            pltpu.VMEM((2, HALO, D), bf),
            dma((4, 4, 2)), dma((4, 4, 2)),
            dma((2, 3, 2)), dma((2, 3, 2)),
            dma((2,)), dma((4, 2)), dma((2,)),
        ],
        compiler_params=pltpu.CompilerParams(
            collective_id=2 if swap else 1, has_side_effects=True
        ),
        name="home_swap" if swap else "home_keep",
    )(*args)


def gates_of(lg, ix):
    experts = lax.broadcasted_iota(jnp.int32, (1, 1, lg.shape[1], 1), 2)
    onehot = (ix[:, :, None, :] == experts).astype(jnp.float32)
    return jax.nn.sigmoid(jnp.sum(onehot * lg[:, None], axis=2)), onehot


def shards(queries, keys, value_sel, expert_logits, expert_index, doc_lengths, group_plan, grad):
    heads = value_sel.shape[1]
    top = value_sel.shape[2]
    vs = lax.optimization_barrier(value_sel.reshape(T, heads * top * D))
    lg = jnp.transpose(expert_logits, (1, 2, 0))
    ix = jnp.transpose(expert_index, (1, 2, 0))
    gates, _ = gates_of(lg, ix)
    flat = jnp.transpose(gates.reshape(heads * top, T))
    wide = vs.astype(jnp.float32)
    mixed = jnp.concatenate(
        [
            flat[:, 2 * h : 2 * h + 1] * wide[:, 2 * h * D : (2 * h + 1) * D]
            + flat[:, 2 * h + 1 : 2 * h + 2] * wide[:, (2 * h + 1) * D : (2 * h + 2) * D]
            for h in range(heads)
        ],
        axis=1,
    ).astype(jnp.bfloat16)

    kh, vh, qh, gh, vs_p, lg_p, ix_p = gather(keys, mixed, queries, grad, vs, lg, ix)

    row = lax.axis_index("seq") // RING
    lengths = doc_lengths[0]
    starts = jnp.cumsum(lengths) - lengths - (row * ROWS - HALO)
    o, dq, dk, dv, dkh, dvh = attend(starts[None].astype(jnp.int32), qh, gh, kh, vh)

    keep = group_plan[0] == 0
    att, dq, dk, gm = lax.cond(
        keep,
        functools.partial(home, False),
        functools.partial(home, True),
        o, dq, dk, dv, dkh, dvh,
    )

    vs_t = jnp.where(keep, vs, vs_p)
    lg_t = jnp.where(keep, lg, lg_p)
    ix_t = jnp.where(keep, ix, ix_p)
    gates, onehot = gates_of(lg_t, ix_t)
    flat = jnp.transpose(gates.reshape(heads * top, T))
    gmf = gm.astype(jnp.float32)
    vsf = vs_t.astype(jnp.float32)
    cols = []
    dots = []
    for i in range(heads * top):
        part = gmf[:, (i // top) * D : (i // top + 1) * D]
        cols.append((flat[:, i : i + 1] * part).astype(jnp.bfloat16))
        dots.append(jnp.sum(part * vsf[:, i * D : (i + 1) * D], axis=1))
    gvs = lax.optimization_barrier(jnp.concatenate(cols, axis=1)).reshape(value_sel.shape)
    gate_grad = jnp.stack(dots, axis=0).reshape(heads, top, T)
    chosen = gate_grad * gates * (1.0 - gates)
    router = jnp.sum(onehot * chosen[:, :, None, :], axis=1)
    return att, dq, dk, gvs, jnp.transpose(router, (2, 0, 1))


def solution(mesh):
    row = P(("dp", "seq"), None)
    cube = P(("dp", "seq"), None, None)
    four = P(("dp", "seq"), None, None, None)
    return jax.shard_map(
        shards,
        mesh=mesh,
        in_specs=(row, row, four, cube, cube, P("dp", None), P(), row),
        out_specs=(row, row, row, four, cube),
        check_vma=False,
    )
```

```python
import functools
import math

import jax
import jax.numpy as jnp
from jax import lax
from jax.experimental import pallas as pl
from jax.experimental.pallas import tpu as pltpu
from jax.sharding import PartitionSpec as P

MESH = pl.DeviceIdType.MESH
ANY = pl.BlockSpec(memory_space=pl.ANY)
RING = 4
T = 512
D = 256
HALO = 3 * T
ROWS = RING * T
SPAN = HALO + ROWS
HALF = T // 2
BQ = 256
CK = 256


def position():
    d = lax.axis_index("dp")
    s = lax.axis_index("seq")
    rows = lax.axis_size("seq") // RING
    return d, lax.rem(s, RING), s // RING, rows


def slab(i):
    return pl.ds(pl.multiple_of(i * D, D), D)


def span(start, size):
    return pl.ds(pl.multiple_of(start, 256), size)


def greet(devices):
    barrier = pltpu.get_barrier_semaphore()
    for device in devices:
        pl.semaphore_signal(barrier, inc=1, device_id=device, device_id_type=MESH)
    pl.semaphore_wait(barrier, len(devices))


def remote(src, dst, send, recv, device):
    return pltpu.make_async_remote_copy(
        src_ref=src,
        dst_ref=dst,
        send_sem=send,
        recv_sem=recv,
        device_id=device,
        device_id_type=MESH,
    )


def nt(a, b):
    return lax.dot_general(a, b, (((1,), (1,)), ((), ())), preferred_element_type=jnp.float32)


def nn(a, b):
    return lax.dot_general(a, b, (((1,), (0,)), ((), ())), preferred_element_type=jnp.float32)


def tn(a, b):
    return lax.dot_general(a, b, (((0,), (0,)), ((), ())), preferred_element_type=jnp.float32)


def gate_rows(lg, ix):
    experts = lax.broadcasted_iota(jnp.int32, (lg.shape[1], lg.shape[2]), 0)
    rows = []
    for h in range(RING):
        for j in range(2):
            chosen = jnp.where(experts == ix[h, j : j + 1, :], lg[h], 0.0)
            rows.append(jax.nn.sigmoid(jnp.sum(chosen, axis=0, keepdims=True)))
    return jnp.concatenate(rows, axis=0)


def core_kernel(
    swap, k, q, g, vs, lg, ix, lengths,
    att_o, dq_o, dk_o, gvs_o, rt_o,
    kb, vb, qb, gb, mixed, vsb, vsp, lgp, ixp, ob, dqb, dka, dva, own, hal, got, gmb, gvb,
    xs, xr, hs, hr, ls, vl, ts, tr, lo, bs, br, gs, ps, pr,
):
    d, x, r, rows = position()
    dest = 1 - d if swap else d
    peers = {o: (d, r * RING + lax.rem(x + o, RING)) for o in (1, 2, 3)}
    down = (d, lax.rem(r + 1, rows) * RING + x)
    up = (d, lax.rem(r + rows - 1, rows) * RING + x)
    partner = (1 - d, r * RING + x)
    near = [peers[1], peers[2], peers[3], down, up]
    if swap:
        near += [(dest, r * RING + lax.rem(x + o, RING)) for o in (0, 1, 2, 3)]
    greet(near)

    srcs = (k, mixed, q, g)
    dsts = (kb, vb, qb, gb)
    bases = (HALO, HALO, 0, 0)

    def x_copy(a, o, c):
        return remote(
            srcs[a].at[pl.ds(c * HALF, HALF), slab(lax.rem(x + o, RING))],
            dsts[a].at[span(bases[a] + x * T + c * HALF, HALF), :],
            xs.at[a, o - 1, c],
            xr.at[a, o - 1, c],
            peers[o],
        )

    def halo_copy(a, j, c):
        return remote(
            dsts[a].at[span(HALO + j * T + c * HALF, HALF), :],
            dsts[a].at[span((j - 1) * T + c * HALF, HALF), :],
            hs.at[a, j - 1, c],
            hr.at[a, j - 1, c],
            down,
        )

    def load_own(a):
        return pltpu.make_async_copy(
            srcs[a].at[:, slab(x)], dsts[a].at[span(bases[a] + x * T, T), :], ls.at[a]
        )

    def relay_own(a):
        for j in (3, 2, 1):

            @pl.when(x == j)
            def _():
                for c in (0, 1):
                    halo_copy(a, j, c).start()

    vs_load = pltpu.make_async_copy(vs, vsb, vl)
    vs_load.start()
    load_own(0).start()
    for c in (0, 1):
        for o in (2, 1, 3):
            x_copy(0, o, c).start()
    swaps = []
    if swap:
        swaps = [
            remote(src, dst, ps.at[i], pr.at[i], partner)
            for i, (src, dst) in enumerate(((vs, vsp), (lg, lgp), (ix, ixp)))
        ]
    gates = gate_rows(lg, ix)
    gate_cols = jnp.transpose(gates)
    load_own(0).wait()
    relay_own(0)
    vs_load.wait()
    for h in range(RING):
        a = vsb[:, 2 * h * D : (2 * h + 1) * D].astype(jnp.float32)
        b = vsb[:, (2 * h + 1) * D : (2 * h + 2) * D].astype(jnp.float32)
        mixed[:, h * D : (h + 1) * D] = (
            gate_cols[:, 2 * h : 2 * h + 1] * a + gate_cols[:, 2 * h + 1 : 2 * h + 2] * b
        ).astype(jnp.bfloat16)
    for c in (0, 1):
        for o in (2, 1, 3):
            x_copy(1, o, c).start()
    load_own(1).start()
    for c in (0, 1):
        for a in (2, 3):
            for o in (2, 1, 3):
                x_copy(a, o, c).start()
    load_own(2).start()
    load_own(3).start()
    for s in swaps:
        s.start()
    load_own(1).wait()
    relay_own(1)
    dka[...] = jnp.zeros_like(dka)
    dva[...] = jnp.zeros_like(dva)

    lens = lengths[...]
    count = lens.shape[1]
    si = lax.broadcasted_iota(jnp.int32, (count, count), 0)
    li = lax.broadcasted_iota(jnp.int32, (count, count), 1)
    col = jnp.sum(jnp.where(li < si, lens, 0), axis=1, keepdims=True)
    starts = jnp.sum(jnp.where(li == si, col, 0), axis=0, keepdims=True) - (r * ROWS - HALO)

    for a in (0, 1):
        for c in (0, 1):
            for o in (1, 3, 2):
                x_copy(a, o, c).wait_recv()
                sender = lax.rem(x + RING - o, RING)
                for j in (3, 2, 1):

                    @pl.when(sender == j)
                    def _():
                        halo_copy(a, j, c).start()

    load_own(2).wait()
    load_own(3).wait()

    outs = (att_o, dq_o, dk_o, gmb)

    def out_src(a, j, c):
        at = span(j * T + c * HALF, HALF)
        return (ob.at[at, :], dqb.at[at, :], own.at[0, at, :], own.at[1, at, :])[a]

    def out_copy(a, j, c):
        i = lax.rem(j - x + RING, RING)
        return remote(
            out_src(a, j, c),
            outs[a].at[pl.ds(c * HALF, HALF), slab(x)],
            ts.at[a, i, c],
            tr.at[a, i, c],
            (dest, r * RING + j),
        )

    def keep_copy(a, c):
        return pltpu.make_async_copy(
            out_src(a, x, c), outs[a].at[pl.ds(c * HALF, HALF), slab(x)], lo.at[a, c]
        )

    def send_home(a, j, c):
        if swap:
            out_copy(a, j, c).start()
            return

        @pl.when(j == x)
        def _():
            keep_copy(a, c).start()

        @pl.when(j != x)
        def _():
            out_copy(a, j, c).start()

    scale = 1.0 / math.sqrt(D)
    width = HALO + BQ

    def attend(b):
        ks = pl.multiple_of(b * BQ, BQ)
        first = HALO + ks
        mine = pl.ds(ks, BQ)
        window = pl.ds(ks, width)
        qq = qb[mine, :]
        gg = gb[mine, :]
        kk = kb[window, :]
        vv = vb[window, :]
        t_col = first + lax.broadcasted_iota(jnp.int32, (BQ, count), 0)
        begin = jnp.max(jnp.where(starts <= t_col, starts, 0), axis=1, keepdims=True)
        t_one = first + lax.broadcasted_iota(jnp.int32, (BQ, 1), 0)
        u = ks + lax.broadcasted_iota(jnp.int32, (BQ, width), 1)
        s = nt(qq, kk) * scale
        s = jnp.where((u >= begin) & (u <= t_one), s, -1e30)
        top = jnp.max(s, axis=1, keepdims=True)
        e = jnp.exp(s - top)
        inv = 1.0 / jnp.sum(e, axis=1, keepdims=True)
        p = e * inv
        low = p.astype(jnp.bfloat16)
        o = nn(low, vv)
        ob[mine, :] = o.astype(jnp.bfloat16)
        delta = jnp.sum(gg.astype(jnp.float32) * o, axis=1, keepdims=True)
        ds = (p * (nt(gg, vv) - delta) * scale).astype(jnp.bfloat16)
        dqb[mine, :] = nn(ds, kk).astype(jnp.bfloat16)
        dka[window, :] += tn(ds, qq)
        dva[window, :] += tn(low, gg)

    def take(j, c):
        @pl.when(j != x)
        def _():
            o = lax.rem(x - j + RING, RING)
            for a in (2, 3):
                remote(
                    srcs[a].at[pl.ds(c * HALF, HALF), slab(x)],
                    dsts[a].at[span(j * T + c * HALF, HALF), :],
                    xs.at[a, o - 1, c],
                    xr.at[a, o - 1, c],
                    (d, r * RING + j),
                ).wait_recv()

    def back_copy(a, j):
        at = span((j - 1) * T, T)
        return remote(hal.at[a, at, :], got.at[a, at, :], bs.at[a, j - 1], br.at[a, j - 1], up)

    def early(i, _):
        j = 3 - i
        take(j, 0)

        @pl.when(i > 0)
        def _():
            for a in (0, 1):
                for c in (0, 1):
                    halo_copy(a, j + 1, c).wait_recv()

        attend(2 * j)
        send_home(0, j, 0)
        send_home(1, j, 0)
        return 0

    def late(j, _):
        take(j, 1)
        attend(2 * j + 1)
        send_home(0, j, 1)
        send_home(1, j, 1)

        @pl.when(j < 3)
        def _():
            at = span(j * T, T)
            hal[0, at, :] = dka[at, :].astype(jnp.bfloat16)
            hal[1, at, :] = dva[at, :].astype(jnp.bfloat16)
            for a in (0, 1):
                back_copy(a, j + 1).start()

        return 0

    lax.fori_loop(0, 4, early, 0)
    lax.fori_loop(0, 4, late, 0)

    own[0, pl.ds(0, T), :] = dka[HALO : HALO + T, :].astype(jnp.bfloat16)
    own[1, pl.ds(0, T), :] = dva[HALO : HALO + T, :].astype(jnp.bfloat16)
    for a in (0, 1):
        for c in (0, 1):
            send_home(a + 2, 0, c)
    if swap:
        for s in swaps:
            s.wait()
        gates = gate_rows(lgp, ixp)
        gate_cols = jnp.transpose(gates)
    values, index = (vsp, ixp) if swap else (vsb, ix)
    for j in (1, 2, 3):
        for a in (0, 1):
            back_copy(a, j).wait_recv()
            part = pl.ds((j - 1) * T, T)
            acc = (dka, dva)[a]
            own[a, pl.ds(j * T, T), :] = (
                acc[HALO + j * T : HALO + (j + 1) * T, :] + got[a, part, :].astype(jnp.float32)
            ).astype(jnp.bfloat16)
            for c in (0, 1):
                send_home(a + 2, j, c)

    def land(a, h, c):
        i = lax.rem(x - h + RING, RING)

        def arrive():
            remote(
                out_src(a, x, c),
                outs[a].at[pl.ds(c * HALF, HALF), pl.ds(h * D, D)],
                ts.at[a, i, c],
                tr.at[a, i, c],
                (dest, r * RING + h),
            ).wait_recv()

        if swap:
            arrive()
            return

        @pl.when(h == x)
        def _():
            keep_copy(a, c).wait()

        @pl.when(h != x)
        def _():
            arrive()

    experts = lax.broadcasted_iota(jnp.int32, (lg.shape[1], HALF), 0)
    for c in (0, 1):
        at = pl.ds(c * HALF, HALF)
        sums = []
        for h in range(RING):
            land(3, h, c)
            part = gmb[at, h * D : (h + 1) * D].astype(jnp.float32)
            for j in (0, 1):
                cols = slice((2 * h + j) * D, (2 * h + j + 1) * D)
                gate = gate_cols[c * HALF : (c + 1) * HALF, 2 * h + j : 2 * h + j + 1]
                gvb[at, cols] = (gate * part).astype(jnp.bfloat16)
                sums.append(
                    jnp.sum(part * values[at, cols].astype(jnp.float32), axis=1, keepdims=True)
                )
        pltpu.make_async_copy(gvb.at[at, :], gvs_o.at[at, :], gs.at[c]).start()
        dots = jnp.transpose(jnp.concatenate(sums, axis=1))
        w = gates[:, c * HALF : (c + 1) * HALF]
        chosen = dots * w * (1.0 - w)
        for h in range(RING):
            total = jnp.zeros(experts.shape, jnp.float32)
            for j in (0, 1):
                hit = experts == index[h, j : j + 1, c * HALF : (c + 1) * HALF]
                total = total + jnp.where(hit, chosen[2 * h + j : 2 * h + j + 1, :], 0.0)
            rt_o[h, :, c * HALF : (c + 1) * HALF] = total

    for c in (0, 1):
        for a in (0, 1, 2):
            for h in range(RING):
                land(a, h, c)
        pltpu.make_async_copy(
            gvb.at[pl.ds(c * HALF, HALF), :], gvs_o.at[pl.ds(c * HALF, HALF), :], gs.at[c]
        ).wait()
    for a in range(4):
        for c in (0, 1):
            for i in range(0 if swap else 1, 4):
                out_copy(a, lax.rem(x + i, RING), c).wait_send()
            for o in (1, 2, 3):
                x_copy(a, o, c).wait_send()
    for a in (0, 1):
        for j in (1, 2, 3):
            back_copy(a, j).wait_send()
            for c in (0, 1):
                halo_copy(a, j, c).wait_send()


def core(swap, k, q, g, vs, lg, ix, lengths):
    bf = jnp.bfloat16
    dma = pltpu.SemaphoreType.DMA
    vmem = pltpu.VMEM
    wide = RING * D
    whole = pl.BlockSpec(memory_space=pltpu.VMEM)

    def body(k, q, g, vs, lg, ix, lengths, *rest):
        core_kernel(swap, k, q, g, vs, lg, ix, lengths, *rest)

    flat = jax.ShapeDtypeStruct((T, wide), bf)
    return pl.pallas_call(
        body,
        out_shape=(
            flat, flat, flat,
            jax.ShapeDtypeStruct(vs.shape, bf),
            jax.ShapeDtypeStruct(lg.shape, jnp.float32),
        ),
        in_specs=[ANY, ANY, ANY, ANY, whole, whole, whole],
        out_specs=[ANY, ANY, ANY, ANY, whole],
        scratch_shapes=[
            vmem((SPAN, D), bf), vmem((SPAN, D), bf), vmem((ROWS, D), bf), vmem((ROWS, D), bf),
            vmem((T, wide), bf), vmem(vs.shape, bf), vmem(vs.shape, bf),
            vmem(lg.shape, lg.dtype), vmem(ix.shape, ix.dtype),
            vmem((ROWS, D), bf), vmem((ROWS, D), bf),
            vmem((SPAN, D), jnp.float32), vmem((SPAN, D), jnp.float32),
            vmem((2, ROWS, D), bf), vmem((2, HALO, D), bf), vmem((2, HALO, D), bf),
            vmem((T, wide), bf), vmem(vs.shape, bf),
            dma((4, 3, 2)), dma((4, 3, 2)), dma((2, 3, 2)), dma((2, 3, 2)),
            dma((4,)), dma, dma((4, 4, 2)), dma((4, 4, 2)), dma((4, 2)),
            dma((2, 3)), dma((2, 3)), dma((2,)), dma((3,)), dma((3,)),
        ],
        compiler_params=pltpu.CompilerParams(
            collective_id=1 if swap else 0,
            has_side_effects=True,
            vmem_limit_bytes=60 * 1024 * 1024,
        ),
        name="core_swap" if swap else "core_keep",
    )(k, q, g, vs, lg, ix, lengths)


def shards(queries, keys, value_sel, expert_logits, expert_index, doc_lengths, group_plan, grad):
    vs = value_sel.reshape(T, -1)
    lg = jnp.transpose(expert_logits, (1, 2, 0))
    ix = jnp.transpose(expert_index, (1, 2, 0))
    att, dq, dk, gvs, router = lax.cond(
        group_plan[0] == 0,
        functools.partial(core, False),
        functools.partial(core, True),
        keys, queries, grad, vs, lg, ix, doc_lengths,
    )
    return att, dq, dk, gvs.reshape(value_sel.shape), jnp.transpose(router, (2, 0, 1))


def solution(mesh):
    row = P(("dp", "seq"), None)
    cube = P(("dp", "seq"), None, None)
    four = P(("dp", "seq"), None, None, None)
    return jax.shard_map(
        shards,
        mesh=mesh,
        in_specs=(row, row, four, cube, cube, P("dp", None), P(), row),
        out_specs=(row, row, row, four, cube),
        check_vma=False,
    )
```

```python
import functools
import math

import jax
import jax.numpy as jnp
from jax import lax
from jax.experimental import pallas as pl
from jax.experimental.pallas import tpu as pltpu
from jax.sharding import PartitionSpec as P

MESH = pl.DeviceIdType.MESH
HBM = pl.BlockSpec(memory_space=pltpu.HBM)
RING = 4
T = 512
D = 256
HALO = 3 * T
ROWS = RING * T
SPAN = HALO + ROWS
HALF = T // 2
PART = 64
BQ = 256
CK = 256


def position():
    d = lax.axis_index("dp")
    s = lax.axis_index("seq")
    rows = lax.axis_size("seq") // RING
    return d, lax.rem(s, RING), s // RING, rows


def slab(i):
    return pl.ds(pl.multiple_of(i * D, D), D)


def span(start, size):
    return pl.ds(pl.multiple_of(start, 256), size)


def greet(devices):
    barrier = pltpu.get_barrier_semaphore()
    for device in devices:
        pl.semaphore_signal(barrier, inc=1, device_id=device, device_id_type=MESH)
    pl.semaphore_wait(barrier, len(devices))


def remote(src, dst, send, recv, device):
    return pltpu.make_async_remote_copy(
        src_ref=src,
        dst_ref=dst,
        send_sem=send,
        recv_sem=recv,
        device_id=device,
        device_id_type=MESH,
    )


def nt(a, b):
    return lax.dot_general(a, b, (((1,), (1,)), ((), ())), preferred_element_type=jnp.float32)


def nn(a, b):
    return lax.dot_general(a, b, (((1,), (0,)), ((), ())), preferred_element_type=jnp.float32)


def tn(a, b):
    return lax.dot_general(a, b, (((0,), (0,)), ((), ())), preferred_element_type=jnp.float32)


def gate_rows(lg, ix):
    experts = lax.broadcasted_iota(jnp.int32, (lg.shape[1], lg.shape[2]), 0)
    rows = []
    for h in range(RING):
        for j in range(2):
            chosen = jnp.where(experts == ix[h, j : j + 1, :], lg[h], 0.0)
            rows.append(jax.nn.sigmoid(jnp.sum(chosen, axis=0, keepdims=True)))
    return jnp.concatenate(rows, axis=0)


def core_kernel(
    swap, k, q, g, vs, lg, ix, lengths,
    att_o, dq_o, dk_o, gvs_o, rt_o,
    kb, vb, qb, gb, mixed, nat, vsb, vsp, lgp, ixp, ob, dqb, dka, dva, own, hal, got, gmb, gcol, grow,
    xs, xr, hs, hr, ls, vl, ts, tr, lo, bs, br, ps, pr,
):
    d, x, r, rows = position()
    dest = 1 - d if swap else d
    peers = {o: (d, r * RING + lax.rem(x + o, RING)) for o in (1, 2, 3)}
    down = (d, lax.rem(r + 1, rows) * RING + x)
    up = (d, lax.rem(r + rows - 1, rows) * RING + x)
    partner = (1 - d, r * RING + x)
    near = [peers[1], peers[2], peers[3], down, up]
    if swap:
        near += [(dest, r * RING + lax.rem(x + o, RING)) for o in (0, 1, 2, 3)]
    greet(near)

    srcs = (k, mixed, q, g)
    dsts = (kb, vb, qb, gb)
    bases = (HALO, HALO, 0, 0)

    def x_copy(a, o, c):
        return remote(
            srcs[a].at[pl.ds(c * HALF, HALF), slab(lax.rem(x + o, RING))],
            dsts[a].at[span(bases[a] + x * T + c * HALF, HALF), :],
            xs.at[a, o - 1, c],
            xr.at[a, o - 1, c],
            peers[o],
        )

    def halo_copy(a, j, c):
        return remote(
            dsts[a].at[span(HALO + j * T + c * HALF, HALF), :],
            dsts[a].at[span((j - 1) * T + c * HALF, HALF), :],
            hs.at[a, j - 1, c],
            hr.at[a, j - 1, c],
            down,
        )

    def load_own(a):
        return pltpu.make_async_copy(
            srcs[a].at[:, slab(x)], dsts[a].at[span(bases[a] + x * T, T), :], ls.at[a]
        )

    def relay_own(a):
        for j in (3, 2, 1):

            @pl.when((x == j) & (r < rows - 1))
            def _():
                for c in (0, 1):
                    halo_copy(a, j, c).start()

    vs_load = pltpu.make_async_copy(vs, nat, vl)
    vs_load.start()
    load_own(0).start()
    for c in (0, 1):
        for o in (1, 3, 2):
            x_copy(0, o, c).start()
    swaps = []
    if swap:
        swaps = [
            remote(src, dst, ps.at[i], pr.at[i], partner)
            for i, (src, dst) in enumerate(((vsb, vsp), (lg, lgp), (ix, ixp)))
        ]
    grow[...] = gate_rows(lg, ix)
    gcol[...] = jnp.transpose(grow[...])
    load_own(0).wait()
    relay_own(0)
    vs_load.wait()
    def blend(c, _):
        at = pl.ds(pl.multiple_of(c * PART, PART), PART)
        pairs = nat[pl.ds(pl.multiple_of(c * PART * RING, PART * RING), PART * RING)]
        pairs = pairs.astype(jnp.float32)
        first, second = (pairs[:, j, :].reshape(PART, RING, D) for j in (0, 1))
        gate = gcol[at, :]
        for h in range(RING):
            one, two = first[:, h, :], second[:, h, :]
            vsb[at, 2 * h * D : (2 * h + 1) * D] = one.astype(jnp.bfloat16)
            vsb[at, (2 * h + 1) * D : (2 * h + 2) * D] = two.astype(jnp.bfloat16)
            mixed[at, h * D : (h + 1) * D] = (
                gate[:, 2 * h : 2 * h + 1] * one + gate[:, 2 * h + 1 : 2 * h + 2] * two
            ).astype(jnp.bfloat16)
        return 0

    lax.fori_loop(0, T // PART, blend, 0)
    for c in (0, 1):
        for o in (1, 3, 2):
            x_copy(1, o, c).start()
    load_own(1).start()
    for c in (0, 1):
        for a in (2, 3):
            for o in (1, 3, 2):
                x_copy(a, o, c).start()
    load_own(2).start()
    load_own(3).start()
    for s in swaps:
        s.start()
    load_own(1).wait()
    relay_own(1)
    dka[...] = jnp.zeros_like(dka)
    dva[...] = jnp.zeros_like(dva)

    @pl.when(r == 0)
    def _():
        kb[:HALO, :] = jnp.zeros((HALO, D), kb.dtype)
        vb[:HALO, :] = jnp.zeros((HALO, D), vb.dtype)

    @pl.when(r == rows - 1)
    def _():
        got[...] = jnp.zeros_like(got)


    lens = lengths[...]
    count = lens.shape[1]
    si = lax.broadcasted_iota(jnp.int32, (count, count), 0)
    li = lax.broadcasted_iota(jnp.int32, (count, count), 1)
    col = jnp.sum(jnp.where(li < si, lens, 0), axis=1, keepdims=True)
    starts = jnp.sum(jnp.where(li == si, col, 0), axis=0, keepdims=True) - (r * ROWS - HALO)

    for a in (0, 1):
        for c in (0, 1):
            for o in (1, 3, 2):
                x_copy(a, o, c).wait_recv()
                sender = lax.rem(x + RING - o, RING)
                for j in (3, 2, 1):

                    @pl.when((sender == j) & (r < rows - 1))
                    def _():
                        halo_copy(a, j, c).start()

    load_own(2).wait()
    load_own(3).wait()

    outs = (att_o, dq_o, dk_o, gmb)

    def out_src(a, j, c):
        at = span(j * T + c * HALF, HALF)
        return (ob.at[at, :], dqb.at[at, :], own.at[0, at, :], own.at[1, at, :])[a]

    def out_copy(a, j, c):
        i = lax.rem(j - x + RING, RING)
        return remote(
            out_src(a, j, c),
            outs[a].at[pl.ds(c * HALF, HALF), slab(x)],
            ts.at[a, i, c],
            tr.at[a, i, c],
            (dest, r * RING + j),
        )

    def keep_copy(a, c):
        return pltpu.make_async_copy(
            out_src(a, x, c), outs[a].at[pl.ds(c * HALF, HALF), slab(x)], lo.at[a, c]
        )

    def send_home(a, j, c):
        if swap:
            out_copy(a, j, c).start()
            return

        @pl.when(j == x)
        def _():
            keep_copy(a, c).start()

        @pl.when(j != x)
        def _():
            out_copy(a, j, c).start()

    scale = 1.0 / math.sqrt(D)
    width = HALO + BQ

    def attend(b):
        ks = pl.multiple_of(b * BQ, BQ)
        first = HALO + ks
        mine = pl.ds(ks, BQ)
        window = pl.ds(ks, width)
        qq = qb[mine, :]
        gg = gb[mine, :]
        kk = kb[window, :]
        vv = vb[window, :]
        t_col = first + lax.broadcasted_iota(jnp.int32, (BQ, count), 0)
        begin = jnp.max(jnp.where(starts <= t_col, starts, 0), axis=1, keepdims=True)
        t_one = first + lax.broadcasted_iota(jnp.int32, (BQ, 1), 0)
        u = ks + lax.broadcasted_iota(jnp.int32, (BQ, width), 1)
        s = nt(qq, kk) * scale
        s = jnp.where((u >= begin) & (u <= t_one), s, -1e30)
        top = jnp.max(s, axis=1, keepdims=True)
        e = jnp.exp(s - top)
        inv = 1.0 / jnp.sum(e, axis=1, keepdims=True)
        p = e * inv
        low = p.astype(jnp.bfloat16)
        o = nn(low, vv)
        ob[mine, :] = o.astype(jnp.bfloat16)
        delta = jnp.sum(gg.astype(jnp.float32) * o, axis=1, keepdims=True)
        ds = (p * (nt(gg, vv) - delta) * scale).astype(jnp.bfloat16)
        dqb[mine, :] = nn(ds, kk).astype(jnp.bfloat16)
        dka[window, :] += tn(ds, qq)
        dva[window, :] += tn(low, gg)

    def take(j, c):
        @pl.when(j != x)
        def _():
            o = lax.rem(x - j + RING, RING)
            for a in (2, 3):
                remote(
                    srcs[a].at[pl.ds(c * HALF, HALF), slab(x)],
                    dsts[a].at[span(j * T + c * HALF, HALF), :],
                    xs.at[a, o - 1, c],
                    xr.at[a, o - 1, c],
                    (d, r * RING + j),
                ).wait_recv()

    def back_copy(a, j, c):
        at = span((j - 1) * T + c * HALF, HALF)
        return remote(
            hal.at[a, at, :], got.at[a, at, :], bs.at[a, j - 1, c], br.at[a, j - 1, c], up
        )

    def early(i, _):
        j = 3 - i
        take(j, 0)

        @pl.when((i > 0) & (r > 0))
        def _():
            for a in (0, 1):
                for c in (0, 1):
                    halo_copy(a, j + 1, c).wait_recv()

        attend(2 * j)
        send_home(0, j, 0)
        send_home(1, j, 0)
        return 0

    def late(j, _):
        take(j, 1)
        attend(2 * j + 1)
        send_home(0, j, 1)
        send_home(1, j, 1)

        @pl.when((j < 3) & (r > 0))
        def _():
            at = span(j * T, T)
            hal[0, at, :] = dka[at, :].astype(jnp.bfloat16)
            hal[1, at, :] = dva[at, :].astype(jnp.bfloat16)
            for a in (0, 1):
                back_copy(a, j + 1, 0).start()

        return 0

    lax.fori_loop(0, 4, early, 0)
    lax.fori_loop(0, 4, late, 0)

    turn = x - x // (RING - 1)
    order = [1 + lax.rem(turn + 1 + i, RING - 1) for i in range(RING - 1)]

    @pl.when(r > 0)
    def _():
        for j in order:
            for a in (0, 1):
                back_copy(a, j, 1).start()

    own[0, pl.ds(0, T), :] = dka[HALO : HALO + T, :].astype(jnp.bfloat16)
    own[1, pl.ds(0, T), :] = dva[HALO : HALO + T, :].astype(jnp.bfloat16)
    if swap:
        for s in swaps:
            s.wait()
        grow[...] = gate_rows(lgp, ixp)
        gcol[...] = jnp.transpose(grow[...])
    values, index = (vsp, ixp) if swap else (vsb, ix)
    for c, blocks in ((0, (1, 2, 3)), (1, order)):
        if c == 1:
            for a in (0, 1):
                for cc in (0, 1):
                    send_home(a + 2, 0, cc)
        for j in blocks:
            for a in (0, 1):

                @pl.when(r < rows - 1)
                def _():
                    back_copy(a, j, c).wait_recv()

                mine = span(j * T + c * HALF, HALF)
                own[a, mine, :] = (
                    (dka, dva)[a][span(HALO + j * T + c * HALF, HALF), :]
                    + got[a, span((j - 1) * T + c * HALF, HALF), :].astype(jnp.float32)
                ).astype(jnp.bfloat16)
                send_home(a + 2, j, c)

    def land(a, h, c):
        i = lax.rem(x - h + RING, RING)

        def arrive():
            remote(
                out_src(a, x, c),
                outs[a].at[pl.ds(c * HALF, HALF), pl.ds(h * D, D)],
                ts.at[a, i, c],
                tr.at[a, i, c],
                (dest, r * RING + h),
            ).wait_recv()

        if swap:
            arrive()
            return

        @pl.when(h == x)
        def _():
            keep_copy(a, c).wait()

        @pl.when(h != x)
        def _():
            arrive()

    experts = lax.broadcasted_iota(jnp.int32, (lg.shape[1], HALF), 0)

    def finish(c, _):
        at = span(c * HALF, HALF)
        sums = []
        gate = gcol[at, :]
        for h in range(RING):
            land(3, h, c)
            part = gmb[at, h * D : (h + 1) * D].astype(jnp.float32)
            pair = []
            for j in (0, 1):
                i = 2 * h + j
                pair.append(gate[:, i : i + 1] * part)
                value = values[at, i * D : (i + 1) * D].astype(jnp.float32)
                sums.append(jnp.sum(part * value, axis=1, keepdims=True))
            gvs_o[at, h, :, :] = jnp.stack(pair, axis=1).astype(jnp.bfloat16)
        dots = jnp.transpose(jnp.concatenate(sums, axis=1))
        w = grow[:, at]
        chosen = dots * w * (1.0 - w)
        for h in range(RING):
            total = jnp.zeros(experts.shape, jnp.float32)
            for j in (0, 1):
                hit = experts == index[h, j : j + 1, at]
                total = total + jnp.where(hit, chosen[2 * h + j : 2 * h + j + 1, :], 0.0)
            rt_o[h, :, at] = total
        return 0

    lax.fori_loop(0, 2, finish, 0)
    for c in (0, 1):
        for a in (0, 1, 2):
            for h in range(RING):
                land(a, h, c)
    for a in range(4):
        for c in (0, 1):
            for i in range(0 if swap else 1, 4):
                out_copy(a, lax.rem(x + i, RING), c).wait_send()
            for o in (1, 2, 3):
                x_copy(a, o, c).wait_send()
    for a in (0, 1):
        for j in (1, 2, 3):
            for c in (0, 1):

                @pl.when(r > 0)
                def _():
                    back_copy(a, j, c).wait_send()

                @pl.when(r < rows - 1)
                def _():
                    halo_copy(a, j, c).wait_send()


def core(swap, k, q, g, vs, lg, ix, lengths):
    bf = jnp.bfloat16
    dma = pltpu.SemaphoreType.DMA
    vmem = pltpu.VMEM
    wide = RING * D
    whole = pl.BlockSpec(memory_space=pltpu.VMEM)

    def body(k, q, g, vs, lg, ix, lengths, *rest):
        core_kernel(swap, k, q, g, vs, lg, ix, lengths, *rest)

    flat = jax.ShapeDtypeStruct((T, wide), bf)
    return pl.pallas_call(
        body,
        out_shape=(
            flat, flat, flat,
            jax.ShapeDtypeStruct((T, RING, 2, D), bf),
            jax.ShapeDtypeStruct(lg.shape, jnp.float32),
        ),
        in_specs=[HBM, HBM, HBM, HBM, whole, whole, whole],
        out_specs=[whole, whole, whole, whole, whole],
        scratch_shapes=[
            vmem((SPAN, D), bf), vmem((SPAN, D), bf), vmem((ROWS, D), bf), vmem((ROWS, D), bf),
            vmem((T, wide), bf), vmem(vs.shape, bf),
            vmem((T, 2 * wide), bf), vmem((T, 2 * wide), bf),
            vmem(lg.shape, lg.dtype), vmem(ix.shape, ix.dtype),
            vmem((ROWS, D), bf), vmem((ROWS, D), bf),
            vmem((SPAN, D), jnp.float32), vmem((SPAN, D), jnp.float32),
            vmem((2, ROWS, D), bf), vmem((2, HALO, D), bf), vmem((2, HALO, D), bf),
            vmem((T, wide), bf), vmem((T, 2 * RING), jnp.float32), vmem((2 * RING, T), jnp.float32),
            dma((4, 3, 2)), dma((4, 3, 2)), dma((2, 3, 2)), dma((2, 3, 2)),
            dma((4,)), dma, dma((4, 4, 2)), dma((4, 4, 2)), dma((4, 2)),
            dma((2, 3, 2)), dma((2, 3, 2)), dma((3,)), dma((3,)),
        ],
        compiler_params=pltpu.CompilerParams(
            collective_id=1 if swap else 0,
            has_side_effects=True,
            vmem_limit_bytes=44 * 1024 * 1024,
        ),
        name="core_swap" if swap else "core_keep",
    )(k, q, g, vs, lg, ix, lengths)


def deliver_kernel(*refs):
    count = (len(refs) - 1) // 2
    sems = refs[-1]
    copies = [
        pltpu.make_async_copy(refs[i], refs[count + i], sems.at[i]) for i in range(count)
    ]
    for copy in copies:
        copy.start()
    for copy in copies:
        copy.wait()


def deliver(*arrays):
    whole = pl.BlockSpec(memory_space=pltpu.VMEM)
    return pl.pallas_call(
        deliver_kernel,
        out_shape=tuple(jax.ShapeDtypeStruct(a.shape, a.dtype) for a in arrays),
        in_specs=[whole] * len(arrays),
        out_specs=[HBM] * len(arrays),
        scratch_shapes=[pltpu.SemaphoreType.DMA((len(arrays),))],
        compiler_params=pltpu.CompilerParams(vmem_limit_bytes=8 * 1024 * 1024),
        name="deliver",
    )(*arrays)


def shards(queries, keys, value_sel, expert_logits, expert_index, doc_lengths, group_plan, grad):
    vs = value_sel.reshape(-1, 2, D)
    lg = jnp.transpose(expert_logits, (1, 2, 0))
    ix = jnp.transpose(expert_index, (1, 2, 0))
    att, dq, dk, gvs, router = lax.cond(
        group_plan[0] == 0,
        functools.partial(core, False),
        functools.partial(core, True),
        keys, queries, grad, vs, lg, ix, doc_lengths,
    )
    att, dq, dk, gvs, router = deliver(att, dq, dk, gvs, router)
    return att, dq, dk, gvs, jnp.transpose(router, (2, 0, 1))


def solution(mesh):
    row = P(("dp", "seq"), None)
    cube = P(("dp", "seq"), None, None)
    four = P(("dp", "seq"), None, None, None)
    return jax.shard_map(
        shards,
        mesh=mesh,
        in_specs=(row, row, four, cube, cube, P("dp", None), P(), row),
        out_specs=(row, row, row, four, cube),
        check_vma=False,
    )
```

```python
import functools
import math

import jax
import jax.numpy as jnp
from jax import lax
from jax.experimental import pallas as pl
from jax.experimental.pallas import tpu as pltpu
from jax.sharding import PartitionSpec as P

MESH = pl.DeviceIdType.MESH
HBM = pl.BlockSpec(memory_space=pltpu.HBM)
RING = 4
T = 512
D = 256
HALO = 3 * T
ROWS = RING * T
SPAN = HALO + ROWS
HALF = T // 2
PART = 64
BQ = 256
CK = 256


def position():
    d = lax.axis_index("dp")
    s = lax.axis_index("seq")
    rows = lax.axis_size("seq") // RING
    return d, lax.rem(s, RING), s // RING, rows


def slab(i):
    return pl.ds(pl.multiple_of(i * D, D), D)


def span(start, size):
    return pl.ds(pl.multiple_of(start, 256), size)


def greet(devices):
    barrier = pltpu.get_barrier_semaphore()
    for device in devices:
        pl.semaphore_signal(barrier, inc=1, device_id=device, device_id_type=MESH)
    pl.semaphore_wait(barrier, len(devices))


def remote(src, dst, send, recv, device):
    return pltpu.make_async_remote_copy(
        src_ref=src,
        dst_ref=dst,
        send_sem=send,
        recv_sem=recv,
        device_id=device,
        device_id_type=MESH,
    )


def nt(a, b):
    return lax.dot_general(a, b, (((1,), (1,)), ((), ())), preferred_element_type=jnp.float32)


def nn(a, b):
    return lax.dot_general(a, b, (((1,), (0,)), ((), ())), preferred_element_type=jnp.float32)


def tn(a, b):
    return lax.dot_general(a, b, (((0,), (0,)), ((), ())), preferred_element_type=jnp.float32)


def gate_rows(lg, ix):
    experts = lax.broadcasted_iota(jnp.int32, (lg.shape[1], lg.shape[2]), 0)
    rows = []
    for h in range(RING):
        for j in range(2):
            chosen = jnp.where(experts == ix[h, j : j + 1, :], lg[h], 0.0)
            rows.append(jax.nn.sigmoid(jnp.sum(chosen, axis=0, keepdims=True)))
    return jnp.concatenate(rows, axis=0)


def core_kernel(
    swap, k, q, g, vs, lg_in, ix_in, len_in,
    att_o, dq_o, dk_o, gvs_o, rt_o,
    kb, vb, qb, gb, mixed, nat, vsb, vsp, lgp, ixp, ob, dqb, dka, dva, own, hal, got, gmb, gcol, grow, lg, ix, lengths,
    xs, xr, hs, hr, ls, vl, ts, tr, lo, bs, br, ps, pr, ss,
):
    d, x, r, rows = position()
    dest = 1 - d if swap else d
    peers = {o: (d, r * RING + lax.rem(x + o, RING)) for o in (1, 2, 3)}
    down = (d, lax.rem(r + 1, rows) * RING + x)
    up = (d, lax.rem(r + rows - 1, rows) * RING + x)
    partner = (1 - d, r * RING + x)
    near = [peers[1], peers[2], peers[3], down, up]
    if swap:
        near += [(dest, r * RING + lax.rem(x + o, RING)) for o in (0, 1, 2, 3)]
    greet(near)

    srcs = (k, mixed, q, g)
    dsts = (kb, vb, qb, gb)
    bases = (HALO, HALO, 0, 0)

    def x_copy(a, o, c):
        return remote(
            srcs[a].at[pl.ds(c * HALF, HALF), slab(lax.rem(x + o, RING))],
            dsts[a].at[span(bases[a] + x * T + c * HALF, HALF), :],
            xs.at[a, o - 1, c],
            xr.at[a, o - 1, c],
            peers[o],
        )

    def halo_copy(a, j, c):
        return remote(
            dsts[a].at[span(HALO + j * T + c * HALF, HALF), :],
            dsts[a].at[span((j - 1) * T + c * HALF, HALF), :],
            hs.at[a, j - 1, c],
            hr.at[a, j - 1, c],
            down,
        )

    def load_own(a):
        return pltpu.make_async_copy(
            srcs[a].at[:, slab(x)], dsts[a].at[span(bases[a] + x * T, T), :], ls.at[a]
        )

    def relay_own(a):
        for j in (3, 2, 1):

            @pl.when((x == j) & (r < rows - 1))
            def _():
                for c in (0, 1):
                    halo_copy(a, j, c).start()

    vs_load = pltpu.make_async_copy(vs, nat, vl)
    for c in (0, 1):
        for o in (1, 3, 2):
            x_copy(0, o, c).start()
    smalls = [
        pltpu.make_async_copy(src, dst, ss.at[i])
        for i, (src, dst) in enumerate(((lg_in, lg), (ix_in, ix), (len_in, lengths)))
    ]
    for small in smalls:
        small.start()
    vs_load.start()
    load_own(0).start()
    for small in smalls:
        small.wait()
    swaps = []
    if swap:
        swaps = [
            remote(src, dst, ps.at[i], pr.at[i], partner)
            for i, (src, dst) in enumerate(((vsb, vsp), (lg, lgp), (ix, ixp)))
        ]
    grow[...] = gate_rows(lg, ix)
    gcol[...] = jnp.transpose(grow[...])
    load_own(0).wait()
    relay_own(0)
    vs_load.wait()
    def blend(c, _):
        at = pl.ds(pl.multiple_of(c * PART, PART), PART)
        pairs = nat[pl.ds(pl.multiple_of(c * PART * RING, PART * RING), PART * RING)]
        pairs = pairs.astype(jnp.float32)
        first, second = (pairs[:, j, :].reshape(PART, RING, D) for j in (0, 1))
        gate = gcol[at, :]
        for h in range(RING):
            one, two = first[:, h, :], second[:, h, :]
            vsb[at, 2 * h * D : (2 * h + 1) * D] = one.astype(jnp.bfloat16)
            vsb[at, (2 * h + 1) * D : (2 * h + 2) * D] = two.astype(jnp.bfloat16)
            mixed[at, h * D : (h + 1) * D] = (
                gate[:, 2 * h : 2 * h + 1] * one + gate[:, 2 * h + 1 : 2 * h + 2] * two
            ).astype(jnp.bfloat16)
        return 0

    lax.fori_loop(0, T // PART, blend, 0)
    for c in (0, 1):
        for o in (1, 3, 2):
            x_copy(1, o, c).start()
    load_own(1).start()
    for c in (0, 1):
        for a in (2, 3):
            for o in (1, 3, 2):
                x_copy(a, o, c).start()
    load_own(2).start()
    load_own(3).start()
    for s in swaps:
        s.start()
    load_own(1).wait()
    relay_own(1)
    dka[...] = jnp.zeros_like(dka)
    dva[...] = jnp.zeros_like(dva)

    @pl.when(r == 0)
    def _():
        kb[:HALO, :] = jnp.zeros((HALO, D), kb.dtype)
        vb[:HALO, :] = jnp.zeros((HALO, D), vb.dtype)

    @pl.when(r == rows - 1)
    def _():
        got[...] = jnp.zeros_like(got)


    lens = lengths[...]
    count = lens.shape[1]
    si = lax.broadcasted_iota(jnp.int32, (count, count), 0)
    li = lax.broadcasted_iota(jnp.int32, (count, count), 1)
    col = jnp.sum(jnp.where(li < si, lens, 0), axis=1, keepdims=True)
    starts = jnp.sum(jnp.where(li == si, col, 0), axis=0, keepdims=True) - (r * ROWS - HALO)

    for a in (0, 1):
        for c in (0, 1):
            for o in (1, 3, 2):
                x_copy(a, o, c).wait_recv()
                sender = lax.rem(x + RING - o, RING)
                for j in (3, 2, 1):

                    @pl.when((sender == j) & (r < rows - 1))
                    def _():
                        halo_copy(a, j, c).start()

    load_own(2).wait()
    load_own(3).wait()

    outs = (att_o, dq_o, dk_o, gmb)

    def out_src(a, j, c):
        at = span(j * T + c * HALF, HALF)
        return (ob.at[at, :], dqb.at[at, :], own.at[0, at, :], own.at[1, at, :])[a]

    def out_copy(a, j, c):
        i = lax.rem(j - x + RING, RING)
        return remote(
            out_src(a, j, c),
            outs[a].at[pl.ds(c * HALF, HALF), slab(x)],
            ts.at[a, i, c],
            tr.at[a, i, c],
            (dest, r * RING + j),
        )

    def keep_copy(a, c):
        return pltpu.make_async_copy(
            out_src(a, x, c), outs[a].at[pl.ds(c * HALF, HALF), slab(x)], lo.at[a, c]
        )

    def send_home(a, j, c):
        if swap:
            out_copy(a, j, c).start()
            return

        @pl.when(j == x)
        def _():
            keep_copy(a, c).start()

        @pl.when(j != x)
        def _():
            out_copy(a, j, c).start()

    scale = 1.0 / math.sqrt(D)
    width = HALO + BQ

    def attend(b):
        ks = pl.multiple_of(b * BQ, BQ)
        first = HALO + ks
        mine = pl.ds(ks, BQ)
        window = pl.ds(ks, width)
        qq = qb[mine, :]
        gg = gb[mine, :]
        kk = kb[window, :]
        vv = vb[window, :]
        t_col = first + lax.broadcasted_iota(jnp.int32, (BQ, count), 0)
        begin = jnp.max(jnp.where(starts <= t_col, starts, 0), axis=1, keepdims=True)
        t_one = first + lax.broadcasted_iota(jnp.int32, (BQ, 1), 0)
        u = ks + lax.broadcasted_iota(jnp.int32, (BQ, width), 1)
        s = nt(qq, kk) * scale
        s = jnp.where((u >= begin) & (u <= t_one), s, -1e30)
        top = jnp.max(s, axis=1, keepdims=True)
        e = jnp.exp(s - top)
        inv = 1.0 / jnp.sum(e, axis=1, keepdims=True)
        p = e * inv
        low = p.astype(jnp.bfloat16)
        o = nn(low, vv)
        ob[mine, :] = o.astype(jnp.bfloat16)
        delta = jnp.sum(gg.astype(jnp.float32) * o, axis=1, keepdims=True)
        ds = (p * (nt(gg, vv) - delta) * scale).astype(jnp.bfloat16)
        dqb[mine, :] = nn(ds, kk).astype(jnp.bfloat16)
        dka[window, :] += tn(ds, qq)
        dva[window, :] += tn(low, gg)

    def take(j, c):
        @pl.when(j != x)
        def _():
            o = lax.rem(x - j + RING, RING)
            for a in (2, 3):
                remote(
                    srcs[a].at[pl.ds(c * HALF, HALF), slab(x)],
                    dsts[a].at[span(j * T + c * HALF, HALF), :],
                    xs.at[a, o - 1, c],
                    xr.at[a, o - 1, c],
                    (d, r * RING + j),
                ).wait_recv()

    def back_copy(a, j, c):
        at = span((j - 1) * T + c * HALF, HALF)
        return remote(
            hal.at[a, at, :], got.at[a, at, :], bs.at[a, j - 1, c], br.at[a, j - 1, c], up
        )

    def early(i, _):
        j = 3 - i
        take(j, 0)

        @pl.when((i > 0) & (r > 0))
        def _():
            for a in (0, 1):
                for c in (0, 1):
                    halo_copy(a, j + 1, c).wait_recv()

        attend(2 * j)
        send_home(0, j, 0)
        send_home(1, j, 0)
        return 0

    def late(j, _):
        take(j, 1)
        attend(2 * j + 1)
        send_home(0, j, 1)
        send_home(1, j, 1)

        @pl.when((j < 3) & (r > 0))
        def _():
            at = span(j * T, T)
            hal[0, at, :] = dka[at, :].astype(jnp.bfloat16)
            hal[1, at, :] = dva[at, :].astype(jnp.bfloat16)
            for a in (1, 0):
                back_copy(a, j + 1, 0).start()

        return 0

    lax.fori_loop(0, 4, early, 0)
    lax.fori_loop(0, 4, late, 0)

    odd = lax.rem(x, 2)
    order = [3, 2 - odd, 1 + odd]

    @pl.when(r > 0)
    def _():
        for j in order:
            for a in (1, 0):
                back_copy(a, j, 1).start()

    own[0, pl.ds(0, T), :] = dka[HALO : HALO + T, :].astype(jnp.bfloat16)
    own[1, pl.ds(0, T), :] = dva[HALO : HALO + T, :].astype(jnp.bfloat16)
    if swap:
        for s in swaps:
            s.wait()
        grow[...] = gate_rows(lgp, ixp)
        gcol[...] = jnp.transpose(grow[...])
    values, index = (vsp, ixp) if swap else (vsb, ix)
    for c, blocks in ((0, (1, 2, 3)), (1, order)):
        if c == 1:
            for a in (0, 1):
                for cc in (0, 1):
                    send_home(a + 2, 0, cc)
        for j in blocks:
            for a in (1, 0):

                @pl.when(r < rows - 1)
                def _():
                    back_copy(a, j, c).wait_recv()

                mine = span(j * T + c * HALF, HALF)
                own[a, mine, :] = (
                    (dka, dva)[a][span(HALO + j * T + c * HALF, HALF), :]
                    + got[a, span((j - 1) * T + c * HALF, HALF), :].astype(jnp.float32)
                ).astype(jnp.bfloat16)
                send_home(a + 2, j, c)

    def land(a, h, c):
        i = lax.rem(x - h + RING, RING)

        def arrive():
            remote(
                out_src(a, x, c),
                outs[a].at[pl.ds(c * HALF, HALF), pl.ds(h * D, D)],
                ts.at[a, i, c],
                tr.at[a, i, c],
                (dest, r * RING + h),
            ).wait_recv()

        if swap:
            arrive()
            return

        @pl.when(h == x)
        def _():
            keep_copy(a, c).wait()

        @pl.when(h != x)
        def _():
            arrive()

    experts = lax.broadcasted_iota(jnp.int32, (lg.shape[1], HALF), 0)

    def finish(c, _):
        at = span(c * HALF, HALF)
        sums = []
        gate = gcol[at, :]
        for h in range(RING):
            land(3, h, c)
            part = gmb[at, h * D : (h + 1) * D].astype(jnp.float32)
            pair = []
            for j in (0, 1):
                i = 2 * h + j
                pair.append(gate[:, i : i + 1] * part)
                value = values[at, i * D : (i + 1) * D].astype(jnp.float32)
                sums.append(jnp.sum(part * value, axis=1, keepdims=True))
            gvs_o[at, h, :, :] = jnp.stack(pair, axis=1).astype(jnp.bfloat16)
        dots = jnp.transpose(jnp.concatenate(sums, axis=1))
        w = grow[:, at]
        chosen = dots * w * (1.0 - w)
        for h in range(RING):
            total = jnp.zeros(experts.shape, jnp.float32)
            for j in (0, 1):
                hit = experts == index[h, j : j + 1, at]
                total = total + jnp.where(hit, chosen[2 * h + j : 2 * h + j + 1, :], 0.0)
            rt_o[h, :, at] = total
        return 0

    lax.fori_loop(0, 2, finish, 0)
    for c in (0, 1):
        for a in (0, 1, 2):
            for h in range(RING):
                land(a, h, c)
    for a in range(4):
        for c in (0, 1):
            for i in range(0 if swap else 1, 4):
                out_copy(a, lax.rem(x + i, RING), c).wait_send()
            for o in (1, 2, 3):
                x_copy(a, o, c).wait_send()
    for a in (0, 1):
        for j in (1, 2, 3):
            for c in (0, 1):

                @pl.when(r > 0)
                def _():
                    back_copy(a, j, c).wait_send()

                @pl.when(r < rows - 1)
                def _():
                    halo_copy(a, j, c).wait_send()


def core(swap, k, q, g, vs, lg, ix, lengths):
    bf = jnp.bfloat16
    dma = pltpu.SemaphoreType.DMA
    vmem = pltpu.VMEM
    wide = RING * D
    whole = pl.BlockSpec(memory_space=pltpu.VMEM)

    def body(k, q, g, vs, lg, ix, lengths, *rest):
        core_kernel(swap, k, q, g, vs, lg, ix, lengths, *rest)

    flat = jax.ShapeDtypeStruct((T, wide), bf)
    return pl.pallas_call(
        body,
        out_shape=(
            flat, flat, flat,
            jax.ShapeDtypeStruct((T, RING, 2, D), bf),
            jax.ShapeDtypeStruct(lg.shape, jnp.float32),
        ),
        in_specs=[HBM] * 7,
        out_specs=[whole, HBM, HBM, whole, whole],
        scratch_shapes=[
            vmem((SPAN, D), bf), vmem((SPAN, D), bf), vmem((ROWS, D), bf), vmem((ROWS, D), bf),
            vmem((T, wide), bf), vmem(vs.shape, bf),
            vmem((T, 2 * wide), bf), vmem((T, 2 * wide), bf),
            vmem(lg.shape, lg.dtype), vmem(ix.shape, ix.dtype),
            vmem((ROWS, D), bf), vmem((ROWS, D), bf),
            vmem((SPAN, D), jnp.float32), vmem((SPAN, D), jnp.float32),
            vmem((2, ROWS, D), bf), vmem((2, HALO, D), bf), vmem((2, HALO, D), bf),
            vmem((T, wide), bf), vmem((T, 2 * RING), jnp.float32), vmem((2 * RING, T), jnp.float32),
            vmem(lg.shape, lg.dtype), vmem(ix.shape, ix.dtype), vmem(lengths.shape, lengths.dtype),
            dma((4, 3, 2)), dma((4, 3, 2)), dma((2, 3, 2)), dma((2, 3, 2)),
            dma((4,)), dma, dma((4, 4, 2)), dma((4, 4, 2)), dma((4, 2)),
            dma((2, 3, 2)), dma((2, 3, 2)), dma((3,)), dma((3,)), dma((3,)),
        ],
        compiler_params=pltpu.CompilerParams(
            collective_id=1 if swap else 0,
            has_side_effects=True,
            vmem_limit_bytes=44 * 1024 * 1024,
        ),
        name="core_swap" if swap else "core_keep",
    )(k, q, g, vs, lg, ix, lengths)


def deliver_kernel(
    att, dq, dk, gvs, rt, att_o, dq_o, dk_o, gvs_o, rt_o, stage, ins, outs, direct
):
    loads = [
        pltpu.make_async_copy(src.at[pl.ds(c * HALF, HALF)], stage.at[a, c], ins.at[a, c])
        for a, src in enumerate((dq, dk))
        for c in (0, 1)
    ]
    stores = [
        pltpu.make_async_copy(stage.at[a, c], dst.at[pl.ds(c * HALF, HALF)], outs.at[a, c])
        for a, dst in enumerate((dq_o, dk_o))
        for c in (0, 1)
    ]
    copies = [
        pltpu.make_async_copy(src, dst, direct.at[i])
        for i, (src, dst) in enumerate(((gvs, gvs_o), (att, att_o), (rt, rt_o)))
    ]
    for copy in loads + copies:
        copy.start()
    for load, store in zip(loads, stores):
        load.wait()
        store.start()
    for copy in copies + stores:
        copy.wait()


def deliver(*arrays):
    whole = pl.BlockSpec(memory_space=pltpu.VMEM)
    dma = pltpu.SemaphoreType.DMA
    return pl.pallas_call(
        deliver_kernel,
        out_shape=tuple(jax.ShapeDtypeStruct(a.shape, a.dtype) for a in arrays),
        in_specs=[whole, HBM, HBM, whole, whole],
        out_specs=[HBM] * len(arrays),
        scratch_shapes=[
            pltpu.VMEM((2, 2, HALF, RING * D), jnp.bfloat16),
            dma((2, 2)), dma((2, 2)), dma((3,)),
        ],
        compiler_params=pltpu.CompilerParams(vmem_limit_bytes=8 * 1024 * 1024),
        name="deliver",
    )(*arrays)


def shards(queries, keys, value_sel, expert_logits, expert_index, doc_lengths, group_plan, grad):
    vs = value_sel.reshape(-1, 2, D)
    lg = jnp.transpose(expert_logits, (1, 2, 0))
    ix = jnp.transpose(expert_index, (1, 2, 0))
    att, dq, dk, gvs, router = lax.cond(
        group_plan[0] == 0,
        functools.partial(core, False),
        functools.partial(core, True),
        keys, queries, grad, vs, lg, ix, doc_lengths,
    )
    att, dq, dk, gvs, router = deliver(att, dq, dk, gvs, router)
    return att, dq, dk, gvs, jnp.transpose(router, (2, 0, 1))


def solution(mesh):
    row = P(("dp", "seq"), None)
    cube = P(("dp", "seq"), None, None)
    four = P(("dp", "seq"), None, None, None)
    return jax.shard_map(
        shards,
        mesh=mesh,
        in_specs=(row, row, four, cube, cube, P("dp", None), P(), row),
        out_specs=(row, row, row, four, cube),
        check_vma=False,
    )
```

```python
import functools
import math

import jax
import jax.numpy as jnp
from jax import lax
from jax.experimental import pallas as pl
from jax.experimental.pallas import tpu as pltpu
from jax.sharding import PartitionSpec as P

MESH = pl.DeviceIdType.MESH
HBM = pl.BlockSpec(memory_space=pltpu.HBM)
RING = 4
T = 512
D = 256
HALO = 3 * T
ROWS = RING * T
SPAN = HALO + ROWS
HALF = T // 2
PART = 64
BQ = 256
CK = 256


def position():
    d = lax.axis_index("dp")
    s = lax.axis_index("seq")
    rows = lax.axis_size("seq") // RING
    return d, lax.rem(s, RING), s // RING, rows


def slab(i):
    return pl.ds(pl.multiple_of(i * D, D), D)


def span(start, size):
    return pl.ds(pl.multiple_of(start, 256), size)


def greet(devices):
    barrier = pltpu.get_barrier_semaphore()
    for device in devices:
        pl.semaphore_signal(barrier, inc=1, device_id=device, device_id_type=MESH)
    pl.semaphore_wait(barrier, len(devices))


def remote(src, dst, send, recv, device):
    return pltpu.make_async_remote_copy(
        src_ref=src,
        dst_ref=dst,
        send_sem=send,
        recv_sem=recv,
        device_id=device,
        device_id_type=MESH,
    )


def nt(a, b):
    return lax.dot_general(a, b, (((1,), (1,)), ((), ())), preferred_element_type=jnp.float32)


def nn(a, b):
    return lax.dot_general(a, b, (((1,), (0,)), ((), ())), preferred_element_type=jnp.float32)


def tn(a, b):
    return lax.dot_general(a, b, (((0,), (0,)), ((), ())), preferred_element_type=jnp.float32)


def gate_rows(lg, ix):
    experts = lax.broadcasted_iota(jnp.int32, (lg.shape[1], lg.shape[2]), 0)
    rows = []
    for h in range(RING):
        for j in range(2):
            chosen = jnp.where(experts == ix[h, j : j + 1, :], lg[h], 0.0)
            rows.append(jax.nn.sigmoid(jnp.sum(chosen, axis=0, keepdims=True)))
    return jnp.concatenate(rows, axis=0)


def core_kernel(
    swap, k, q, g, vs, lg_in, ix_in, len_in,
    att_o, dq_o, dk_o, gvs_o, rt_o,
    kb, vb, qb, gb, mixed, nat, vsb, vsp, lgp, ixp, ob, dqb, dka, dva, own, hal, got, gmb, gcol, grow, lg, ix, lengths,
    xs, xr, hs, hr, ls, vl, ts, tr, lo, bs, br, ps, pr, ss,
):
    d, x, r, rows = position()
    dest = 1 - d if swap else d
    peers = {o: (d, r * RING + lax.rem(x + o, RING)) for o in (1, 2, 3)}
    down = (d, lax.rem(r + 1, rows) * RING + x)
    up = (d, lax.rem(r + rows - 1, rows) * RING + x)
    partner = (1 - d, r * RING + x)
    near = [peers[1], peers[2], peers[3], down, up]
    if swap:
        near += [(dest, r * RING + lax.rem(x + o, RING)) for o in (0, 1, 2, 3)]
    greet(near)

    srcs = (k, mixed, q, g)
    dsts = (kb, vb, qb, gb)
    bases = (HALO, HALO, 0, 0)

    def x_copy(a, o, c):
        return remote(
            srcs[a].at[pl.ds(c * HALF, HALF), slab(lax.rem(x + o, RING))],
            dsts[a].at[span(bases[a] + x * T + c * HALF, HALF), :],
            xs.at[a, o - 1, c],
            xr.at[a, o - 1, c],
            peers[o],
        )

    def halo_copy(a, j, c):
        return remote(
            dsts[a].at[span(HALO + j * T + c * HALF, HALF), :],
            dsts[a].at[span((j - 1) * T + c * HALF, HALF), :],
            hs.at[a, j - 1, c],
            hr.at[a, j - 1, c],
            down,
        )

    def load_own(a):
        return pltpu.make_async_copy(
            srcs[a].at[:, slab(x)], dsts[a].at[span(bases[a] + x * T, T), :], ls.at[a]
        )

    def relay_own(a):
        for j in (3, 2, 1):

            @pl.when((x == j) & (r < rows - 1))
            def _():
                for c in (0, 1):
                    halo_copy(a, j, c).start()

    vs_load = pltpu.make_async_copy(vs, nat, vl)
    for c in (0, 1):
        for o in (1, 3, 2):
            x_copy(0, o, c).start()
    smalls = [
        pltpu.make_async_copy(src, dst, ss.at[i])
        for i, (src, dst) in enumerate(((lg_in, lg), (ix_in, ix), (len_in, lengths)))
    ]
    for small in smalls:
        small.start()
    vs_load.start()
    load_own(0).start()
    for small in smalls:
        small.wait()
    swaps = []
    if swap:
        swaps = [
            remote(src, dst, ps.at[i], pr.at[i], partner)
            for i, (src, dst) in enumerate(((vsb, vsp), (lg, lgp), (ix, ixp)))
        ]
    grow[...] = gate_rows(lg, ix)
    gcol[...] = jnp.transpose(grow[...])
    load_own(0).wait()
    relay_own(0)
    vs_load.wait()
    def blend(c, _):
        at = pl.ds(pl.multiple_of(c * PART, PART), PART)
        pairs = nat[pl.ds(pl.multiple_of(c * PART * RING, PART * RING), PART * RING)]
        pairs = pairs.astype(jnp.float32)
        first, second = (pairs[:, j, :].reshape(PART, RING, D) for j in (0, 1))
        gate = gcol[at, :]
        for h in range(RING):
            one, two = first[:, h, :], second[:, h, :]
            vsb[at, 2 * h * D : (2 * h + 1) * D] = one.astype(jnp.bfloat16)
            vsb[at, (2 * h + 1) * D : (2 * h + 2) * D] = two.astype(jnp.bfloat16)
            mixed[at, h * D : (h + 1) * D] = (
                gate[:, 2 * h : 2 * h + 1] * one + gate[:, 2 * h + 1 : 2 * h + 2] * two
            ).astype(jnp.bfloat16)
        return 0

    lax.fori_loop(0, T // PART, blend, 0)
    for c in (0, 1):
        for o in (1, 3, 2):
            x_copy(1, o, c).start()
    load_own(1).start()
    for c in (0, 1):
        for a in (2, 3):
            for o in (1, 3, 2):
                x_copy(a, o, c).start()
    load_own(2).start()
    load_own(3).start()
    for s in swaps:
        s.start()
    load_own(1).wait()
    relay_own(1)
    dka[...] = jnp.zeros_like(dka)
    dva[...] = jnp.zeros_like(dva)

    @pl.when(r == 0)
    def _():
        kb[:HALO, :] = jnp.zeros((HALO, D), kb.dtype)
        vb[:HALO, :] = jnp.zeros((HALO, D), vb.dtype)

    @pl.when(r == rows - 1)
    def _():
        got[...] = jnp.zeros_like(got)


    lens = lengths[...]
    count = lens.shape[1]
    si = lax.broadcasted_iota(jnp.int32, (count, count), 0)
    li = lax.broadcasted_iota(jnp.int32, (count, count), 1)
    col = jnp.sum(jnp.where(li < si, lens, 0), axis=1, keepdims=True)
    starts = jnp.sum(jnp.where(li == si, col, 0), axis=0, keepdims=True) - (r * ROWS - HALO)

    for a in (0, 1):
        for c in (0, 1):
            for o in (1, 3, 2):
                x_copy(a, o, c).wait_recv()
                sender = lax.rem(x + RING - o, RING)
                for j in (3, 2, 1):

                    @pl.when((sender == j) & (r < rows - 1))
                    def _():
                        halo_copy(a, j, c).start()

    load_own(2).wait()
    load_own(3).wait()

    outs = (att_o, dq_o, dk_o, gmb)

    def out_src(a, j, c):
        at = span(j * T + c * HALF, HALF)
        return (ob.at[at, :], dqb.at[at, :], own.at[0, at, :], own.at[1, at, :])[a]

    def out_copy(a, j, c):
        i = lax.rem(j - x + RING, RING)
        return remote(
            out_src(a, j, c),
            outs[a].at[pl.ds(c * HALF, HALF), slab(x)],
            ts.at[a, i, c],
            tr.at[a, i, c],
            (dest, r * RING + j),
        )

    def keep_copy(a, c):
        return pltpu.make_async_copy(
            out_src(a, x, c), outs[a].at[pl.ds(c * HALF, HALF), slab(x)], lo.at[a, c]
        )

    def send_home(a, j, c):
        if swap:
            out_copy(a, j, c).start()
            return

        @pl.when(j == x)
        def _():
            keep_copy(a, c).start()

        @pl.when(j != x)
        def _():
            out_copy(a, j, c).start()

    scale = 1.0 / math.sqrt(D)
    width = HALO + BQ

    def attend(b, j, c):
        ks = pl.multiple_of(b * BQ, BQ)
        first = HALO + ks
        mine = pl.ds(ks, BQ)
        window = pl.ds(ks, width)
        qq = qb[mine, :]
        gg = gb[mine, :]
        kk = kb[window, :]
        vv = vb[window, :]
        t_col = first + lax.broadcasted_iota(jnp.int32, (BQ, count), 0)
        begin = jnp.max(jnp.where(starts <= t_col, starts, 0), axis=1, keepdims=True)
        t_one = first + lax.broadcasted_iota(jnp.int32, (BQ, 1), 0)
        u = ks + lax.broadcasted_iota(jnp.int32, (BQ, width), 1)
        s = nt(qq, kk) * scale
        s = jnp.where((u >= begin) & (u <= t_one), s, -1e30)
        top = jnp.max(s, axis=1, keepdims=True)
        e = jnp.exp(s - top)
        inv = 1.0 / jnp.sum(e, axis=1, keepdims=True)
        p = e * inv
        low = p.astype(jnp.bfloat16)
        o = nn(low, vv)
        ob[mine, :] = o.astype(jnp.bfloat16)
        send_home(0, j, c)
        delta = jnp.sum(gg.astype(jnp.float32) * o, axis=1, keepdims=True)
        ds = (p * (nt(gg, vv) - delta) * scale).astype(jnp.bfloat16)
        dqb[mine, :] = nn(ds, kk).astype(jnp.bfloat16)
        send_home(1, j, c)
        dka[window, :] += tn(ds, qq)
        dva[window, :] += tn(low, gg)

    def take(j, c):
        @pl.when(j != x)
        def _():
            o = lax.rem(x - j + RING, RING)
            for a in (2, 3):
                remote(
                    srcs[a].at[pl.ds(c * HALF, HALF), slab(x)],
                    dsts[a].at[span(j * T + c * HALF, HALF), :],
                    xs.at[a, o - 1, c],
                    xr.at[a, o - 1, c],
                    (d, r * RING + j),
                ).wait_recv()

    def back_copy(a, j, c):
        at = span((j - 1) * T + c * HALF, HALF)
        return remote(
            hal.at[a, at, :], got.at[a, at, :], bs.at[a, j - 1, c], br.at[a, j - 1, c], up
        )

    def early(i, _):
        j = 3 - i
        take(j, 0)

        @pl.when((i > 0) & (r > 0))
        def _():
            for a in (0, 1):
                for c in (0, 1):
                    halo_copy(a, j + 1, c).wait_recv()

        attend(2 * j, j, 0)
        return 0

    def late(j, _):
        take(j, 1)
        attend(2 * j + 1, j, 1)

        @pl.when((j < 3) & (r > 0))
        def _():
            at = span(j * T, T)
            hal[0, at, :] = dka[at, :].astype(jnp.bfloat16)
            hal[1, at, :] = dva[at, :].astype(jnp.bfloat16)
            for a in (1, 0):
                back_copy(a, j + 1, 0).start()

        return 0

    lax.fori_loop(0, 4, early, 0)
    lax.fori_loop(0, 4, late, 0)

    odd = lax.rem(x, 2)
    order = [3, 2 - odd, 1 + odd]

    @pl.when(r > 0)
    def _():
        for j in order:
            for a in (1, 0):
                back_copy(a, j, 1).start()

    own[0, pl.ds(0, T), :] = dka[HALO : HALO + T, :].astype(jnp.bfloat16)
    own[1, pl.ds(0, T), :] = dva[HALO : HALO + T, :].astype(jnp.bfloat16)
    if swap:
        for s in swaps:
            s.wait()
        grow[...] = gate_rows(lgp, ixp)
        gcol[...] = jnp.transpose(grow[...])
    values, index = (vsp, ixp) if swap else (vsb, ix)
    def land(a, h, c):
        i = lax.rem(x - h + RING, RING)

        def arrive():
            remote(
                out_src(a, x, c),
                outs[a].at[pl.ds(c * HALF, HALF), pl.ds(h * D, D)],
                ts.at[a, i, c],
                tr.at[a, i, c],
                (dest, r * RING + h),
            ).wait_recv()

        if swap:
            arrive()
            return

        @pl.when(h == x)
        def _():
            keep_copy(a, c).wait()

        @pl.when(h != x)
        def _():
            arrive()

    experts = lax.broadcasted_iota(jnp.int32, (lg.shape[1], HALF), 0)

    def finish(c, _):
        at = span(c * HALF, HALF)
        sums = []
        gate = gcol[at, :]
        for h in range(RING):
            land(3, h, c)
            part = gmb[at, h * D : (h + 1) * D].astype(jnp.float32)
            pair = []
            for j in (0, 1):
                i = 2 * h + j
                pair.append(gate[:, i : i + 1] * part)
                value = values[at, i * D : (i + 1) * D].astype(jnp.float32)
                sums.append(jnp.sum(part * value, axis=1, keepdims=True))
            gvs_o[at, h, :, :] = jnp.stack(pair, axis=1).astype(jnp.bfloat16)
        dots = jnp.transpose(jnp.concatenate(sums, axis=1))
        w = grow[:, at]
        chosen = dots * w * (1.0 - w)
        for h in range(RING):
            total = jnp.zeros(experts.shape, jnp.float32)
            for j in (0, 1):
                hit = experts == index[h, j : j + 1, at]
                total = total + jnp.where(hit, chosen[2 * h + j : 2 * h + j + 1, :], 0.0)
            rt_o[h, :, at] = total
        return 0

    for c, blocks in ((0, (1, 2, 3)), (1, order)):
        if c == 1:
            for a in (1, 0):
                for cc in (0, 1):
                    send_home(a + 2, 0, cc)
        for n, j in enumerate(blocks):
            if c == 1 and n == 2:
                finish(0, 0)
            for a in (1, 0):

                @pl.when(r < rows - 1)
                def _():
                    back_copy(a, j, c).wait_recv()

                mine = span(j * T + c * HALF, HALF)
                own[a, mine, :] = (
                    (dka, dva)[a][span(HALO + j * T + c * HALF, HALF), :]
                    + got[a, span((j - 1) * T + c * HALF, HALF), :].astype(jnp.float32)
                ).astype(jnp.bfloat16)
                send_home(a + 2, j, c)

    finish(1, 0)
    for c in (0, 1):
        for a in (0, 1, 2):
            for h in range(RING):
                land(a, h, c)
    for a in range(4):
        for c in (0, 1):
            for i in range(0 if swap else 1, 4):
                out_copy(a, lax.rem(x + i, RING), c).wait_send()
            for o in (1, 2, 3):
                x_copy(a, o, c).wait_send()
    for a in (0, 1):
        for j in (1, 2, 3):
            for c in (0, 1):

                @pl.when(r > 0)
                def _():
                    back_copy(a, j, c).wait_send()

                @pl.when(r < rows - 1)
                def _():
                    halo_copy(a, j, c).wait_send()


def core(swap, k, q, g, vs, lg, ix, lengths):
    bf = jnp.bfloat16
    dma = pltpu.SemaphoreType.DMA
    vmem = pltpu.VMEM
    wide = RING * D
    whole = pl.BlockSpec(memory_space=pltpu.VMEM)

    def body(k, q, g, vs, lg, ix, lengths, *rest):
        core_kernel(swap, k, q, g, vs, lg, ix, lengths, *rest)

    flat = jax.ShapeDtypeStruct((T, wide), bf)
    return pl.pallas_call(
        body,
        out_shape=(
            flat, flat, flat,
            jax.ShapeDtypeStruct((T, RING, 2, D), bf),
            jax.ShapeDtypeStruct(lg.shape, jnp.float32),
        ),
        in_specs=[HBM] * 7,
        out_specs=[whole, HBM, HBM, whole, whole],
        scratch_shapes=[
            vmem((SPAN, D), bf), vmem((SPAN, D), bf), vmem((ROWS, D), bf), vmem((ROWS, D), bf),
            vmem((T, wide), bf), vmem(vs.shape, bf),
            vmem((T, 2 * wide), bf), vmem((T, 2 * wide), bf),
            vmem(lg.shape, lg.dtype), vmem(ix.shape, ix.dtype),
            vmem((ROWS, D), bf), vmem((ROWS, D), bf),
            vmem((SPAN, D), jnp.float32), vmem((SPAN, D), jnp.float32),
            vmem((2, ROWS, D), bf), vmem((2, HALO, D), bf), vmem((2, HALO, D), bf),
            vmem((T, wide), bf), vmem((T, 2 * RING), jnp.float32), vmem((2 * RING, T), jnp.float32),
            vmem(lg.shape, lg.dtype), vmem(ix.shape, ix.dtype), vmem(lengths.shape, lengths.dtype),
            dma((4, 3, 2)), dma((4, 3, 2)), dma((2, 3, 2)), dma((2, 3, 2)),
            dma((4,)), dma, dma((4, 4, 2)), dma((4, 4, 2)), dma((4, 2)),
            dma((2, 3, 2)), dma((2, 3, 2)), dma((3,)), dma((3,)), dma((3,)),
        ],
        compiler_params=pltpu.CompilerParams(
            collective_id=1 if swap else 0,
            has_side_effects=True,
            vmem_limit_bytes=44 * 1024 * 1024,
        ),
        name="core_swap" if swap else "core_keep",
    )(k, q, g, vs, lg, ix, lengths)


def deliver_kernel(
    att, dq, dk, gvs, rt, att_o, dq_o, dk_o, gvs_o, rt_o, stage, ins, outs, direct
):
    loads = [
        pltpu.make_async_copy(src.at[pl.ds(c * HALF, HALF)], stage.at[a, c], ins.at[a, c])
        for a, src in enumerate((dq, dk))
        for c in (0, 1)
    ]
    stores = [
        pltpu.make_async_copy(stage.at[a, c], dst.at[pl.ds(c * HALF, HALF)], outs.at[a, c])
        for a, dst in enumerate((dq_o, dk_o))
        for c in (0, 1)
    ]
    copies = [
        pltpu.make_async_copy(src, dst, direct.at[i])
        for i, (src, dst) in enumerate(((gvs, gvs_o), (att, att_o), (rt, rt_o)))
    ]
    for i, copy in enumerate(loads + copies):
        copy.start(priority=i % 2)
    for i, (load, store) in enumerate(zip(loads, stores)):
        load.wait()
        store.start(priority=i % 2)
    for copy in copies + stores:
        copy.wait()


def deliver(*arrays):
    whole = pl.BlockSpec(memory_space=pltpu.VMEM)
    dma = pltpu.SemaphoreType.DMA
    return pl.pallas_call(
        deliver_kernel,
        out_shape=tuple(jax.ShapeDtypeStruct(a.shape, a.dtype) for a in arrays),
        in_specs=[whole, HBM, HBM, whole, whole],
        out_specs=[HBM] * len(arrays),
        scratch_shapes=[
            pltpu.VMEM((2, 2, HALF, RING * D), jnp.bfloat16),
            dma((2, 2)), dma((2, 2)), dma((3,)),
        ],
        compiler_params=pltpu.CompilerParams(vmem_limit_bytes=8 * 1024 * 1024),
        name="deliver",
    )(*arrays)


def shards(queries, keys, value_sel, expert_logits, expert_index, doc_lengths, group_plan, grad):
    vs = value_sel.reshape(-1, 2, D)
    lg = jnp.transpose(expert_logits, (1, 2, 0))
    ix = jnp.transpose(expert_index, (1, 2, 0))
    att, dq, dk, gvs, router = lax.cond(
        group_plan[0] == 0,
        functools.partial(core, False),
        functools.partial(core, True),
        keys, queries, grad, vs, lg, ix, doc_lengths,
    )
    att, dq, dk, gvs, router = deliver(att, dq, dk, gvs, router)
    return att, dq, dk, gvs, jnp.transpose(router, (2, 0, 1))


def solution(mesh):
    row = P(("dp", "seq"), None)
    cube = P(("dp", "seq"), None, None)
    four = P(("dp", "seq"), None, None, None)
    return jax.shard_map(
        shards,
        mesh=mesh,
        in_specs=(row, row, four, cube, cube, P("dp", None), P(), row),
        out_specs=(row, row, row, four, cube),
        check_vma=False,
    )
```
